128 devices in a mesh: group: 4 (over x), dev: 32 (over y, z, core).
Axes of the slice: x: 4, y: 4, z: 4, core: 2. Of those that a mesh axis runs over, the one named last changes fastest.
Arguments:
- node_feats: bfloat16 [32768, 1024], P(('group', 'dev')), may hold values from -60 to 60
- w_gcn: bfloat16 [1024, 1024], replicated, may hold values from -0.1875 to 0.1875
- adj_tiles: bfloat16 [256, 16, 128, 128], P(('group', 'dev')), may hold values from -0.125 to 0.125
- neighbor_blocks: int32 [256, 16], P(('group', 'dev')), may hold values from 0 to 21, all different within a row
- inner_rows: int32 [128, 32, 64], P(('group', 'dev')), may hold values from 0 to 255
- outer_rows: int32 [128, 4, 128], P(('group', 'dev')), may hold values from 0 to 255
- w_qkv: bfloat16 [1024, 3072], replicated, may hold values from -0.1875 to 0.1875
- key_blocks: int32 [256, 16], P('group'), may hold values from 0 to 63, all different within a row
- key_counts: int32 [256], P('group'), may hold values from 1 to 16
- w_out: bfloat16 [1024, 1024], replicated, may hold values from -0.1875 to 0.1875
- w_up: bfloat16 [1024, 2048], replicated, may hold values from -0.1875 to 0.1875
- w_down: bfloat16 [2048, 1024], replicated, may hold values from -0.125 to 0.125
Outputs:
- layer_out: bfloat16 [32768, 1024], P(('group', 'dev'))
The draws below stay inside these ranges and needn't reach their ends.
Inputs may be any that keep to these rules, and one draw needn't show every extreme that they name: `inner_rows`: row numbers of the sending device. `outer_rows`: row numbers of the sending device. `neighbor_blocks`: table block numbers; the 16 entries of a row differ. `key_blocks`: the 16 entries of a row differ.
All inputs are finite; a program needn't handle non-finite values.
Results may differ from the reference program's by a relative error of at most 0.012.
The reference program's roundings to bfloat16 on the way count: a program that leaves them out, or rounds other values in their place, can miss the bound.
Values may be sent and summed in bfloat16 or wider, within the bound.
A program may use at most 128 MiB of HBM per device.

```python
import jax
import jax.numpy as jnp
from jax import lax

D = 1024
H = 32
HD = 32
FF = 2048
BLOCK = 128
BLK_DEV = 2
NBR = 16
KB = 16
ROWS_DEV = 256
NODES = 32768
NODE_BLKS = 256
QB_G = 64
IN_SLOT = 64
X_SLOT = 128
TAB_BLK = 22
N_GROUP = 4
N_DEV = 32
DEVICES = 128


def draw_node_feats(key, part):
    first_key = jax.random.fold_in(jax.random.fold_in(key, 11), 0)
    values = jnp.clip(jax.random.normal(first_key, (NODES, D), jnp.float32), -6.0, 6.0)
    return values.astype(jnp.bfloat16)


def set_ends(array, own_key, smallest, largest):
    dims = array.shape
    place = [jax.random.randint(jax.random.fold_in(own_key, axis), (), 0, dims[axis]) for axis in range(len(dims))]
    array = array.at[tuple(place)].set(smallest)
    longest = dims.index(max(dims))
    place[longest] = (place[longest] + 1) % dims[longest]
    return array.at[tuple(place)].set(largest)


def steps_of(rng, shape, cuts, low, top_value):
    level = 1.0
    for axis_at, shards_of in cuts:
        steps = jax.random.uniform(jax.random.fold_in(jax.random.fold_in(rng, 6), axis_at), (shards_of,), jnp.float32, low / len(cuts), top_value / len(cuts))
        level = level * jnp.repeat(jnp.exp(steps), shape[axis_at] // shards_of).reshape((-1,) + (1,) * (len(shape) - 1 - axis_at))
    return level


def picks_of(key, rows, amount, top, lift):
    ranking = jax.random.permutation(jax.random.fold_in(key, 1), amount)
    favour = ranking
    for power in range(3):
        favour = favour * favour // amount
    favour = favour * lift // amount
    tickets = jax.random.randint(jax.random.fold_in(key, 2), (rows, amount), 0, 4096) + favour
    holders = jax.random.permutation(jax.random.fold_in(key, 3), rows)[jnp.arange(amount) % rows]
    tickets = jnp.where(jnp.arange(rows)[:, None] == holders[None, :], 1 << 14, tickets)
    merit = tickets * amount + jnp.arange(amount)
    return lax.top_k(merit.astype(jnp.int32), top)[1].astype(jnp.int32)


def noise(own_key, dims, width, most, pieces=(), kind=jnp.bfloat16):
    values = jax.random.normal(own_key, dims, jnp.float32) * width
    if len(pieces) > 0:
        values = steps_of(own_key, dims, pieces, -0.22, 0.18) * values
    return jnp.clip(values, min=-most, max=most).astype(kind)


def setup_inputs(seed: int = 0) -> dict:
    arg_keys = jax.random.split(jax.random.key(seed), 13)
    return {
        "node_feats": draw_node_feats(jax.random.fold_in(arg_keys[12], 71), 0),
        "w_gcn": noise(arg_keys[1], (D, D), D ** -0.5, 0.1875),
        "adj_tiles": noise(arg_keys[2], (NODE_BLKS, NBR, BLOCK, BLOCK), (NBR * BLOCK) ** -0.5, 0.125, ((0, 128),)),
        "neighbor_blocks": picks_of(arg_keys[3], NODE_BLKS, TAB_BLK, NBR, 0),
        "inner_rows": set_ends(jax.random.randint(arg_keys[4], (DEVICES, N_DEV, IN_SLOT), 0, ROWS_DEV), jax.random.fold_in(arg_keys[4], 1), 0, ROWS_DEV - 1).astype(jnp.int32),
        "outer_rows": set_ends(jax.random.randint(arg_keys[5], (DEVICES, N_GROUP, X_SLOT), 0, ROWS_DEV), jax.random.fold_in(arg_keys[5], 1), 0, ROWS_DEV - 1).astype(jnp.int32),
        "w_qkv": noise(arg_keys[6], (D, 3 * D), D ** -0.5, 0.1875),
        "key_blocks": picks_of(arg_keys[7], (N_GROUP * QB_G), QB_G, KB, 0),
        "key_counts": set_ends(jax.random.randint(arg_keys[8], (N_GROUP * QB_G,), 1, KB + 1), jax.random.fold_in(arg_keys[8], 1), 1, KB).astype(jnp.int32),
        "w_out": noise(arg_keys[9], (D, D), D ** -0.5, 0.1875),
        "w_up": noise(arg_keys[10], (D, FF), D ** -0.5, 0.1875),
        "w_down": noise(arg_keys[11], (FF, D), FF ** -0.5, 0.125),
    }


def layer_norm(values):
    average = lax.optimization_barrier(jnp.mean(values, axis=-1, keepdims=True))
    centered = values - average
    variance = lax.optimization_barrier(jnp.mean(centered * centered, axis=-1, keepdims=True))
    return centered / jnp.sqrt(variance + 1e-05)

def reference(node_feats, w_gcn, adj_tiles, neighbor_blocks, inner_rows, outer_rows, w_qkv, key_blocks, key_counts, w_out, w_up, w_down):
    device_total = N_GROUP * N_DEV
    gcn_rows = jnp.dot(node_feats, w_gcn, preferred_element_type=jnp.float32).astype(jnp.bfloat16)
    device_ids = jnp.arange(device_total, dtype=jnp.int32)
    group_of = device_ids // N_DEV
    dev_place = device_ids % N_DEV
    own_rows = device_ids[:, None] * ROWS_DEV + jnp.arange(ROWS_DEV, dtype=jnp.int32)[None, :]
    senders = group_of[:, None] * N_DEV + jnp.arange(N_DEV, dtype=jnp.int32)[None, :]
    inner_local = inner_rows[senders, dev_place[:, None], :]
    inner_global = senders[:, :, None] * ROWS_DEV + inner_local
    far_senders = jnp.arange(N_GROUP, dtype=jnp.int32)[None, :] * N_DEV + dev_place[:, None]
    outer_local = outer_rows[far_senders, group_of[:, None], :]
    outer_global = far_senders[:, :, None] * ROWS_DEV + outer_local
    table_index = jnp.concatenate([own_rows, inner_global.reshape(device_total, -1), outer_global.reshape(device_total, -1)], axis=1).astype(jnp.int32)
    table_blocks = table_index.reshape(device_total, TAB_BLK, BLOCK)

    def aggregate(inputs):
        block_id, slots, tile_set = inputs
        owner = block_id // BLK_DEV
        source_rows = table_blocks[owner][slots]
        source = gcn_rows[source_rows]
        return jnp.einsum('sij,sjd->id', tile_set.astype(jnp.float32), source.astype(jnp.float32))
    agg = lax.map(aggregate, (jnp.arange(NODE_BLKS, dtype=jnp.int32), neighbor_blocks, adj_tiles))
    agg = agg.reshape(NODES, D)
    features = node_feats.astype(jnp.float32)
    local_branch = layer_norm(features + agg)
    qkv = jnp.dot(node_feats, w_qkv, preferred_element_type=jnp.float32).astype(jnp.bfloat16)
    query_blocks = qkv[:, :D].reshape(NODE_BLKS, BLOCK, H, HD)
    key_rows = qkv[:, D:2 * D].reshape(NODE_BLKS, BLOCK, H, HD)
    value_rows = qkv[:, 2 * D:].reshape(NODE_BLKS, BLOCK, H, HD)
    scale = 1.0 / HD ** 0.5

    def attend(inputs):
        block_ids, picks, counts = inputs
        base = block_ids // QB_G * QB_G
        chosen = (base[:, None] + picks).astype(jnp.int32)
        queries = query_blocks[block_ids].astype(jnp.float32)
        keys_here = key_rows[chosen].astype(jnp.float32)
        values_here = value_rows[chosen].astype(jnp.float32)
        scores = jnp.einsum('qihe,qsjhe->qhisj', queries, keys_here) * scale
        live = jnp.arange(KB, dtype=jnp.int32)[None, :] < counts[:, None]
        scores = jnp.where(live[:, None, None, :, None], scores, -jnp.inf)
        highest = lax.optimization_barrier(jnp.max(scores, axis=(3, 4), keepdims=True))
        expos = jnp.exp(scores - highest)
        totals = lax.optimization_barrier(jnp.sum(expos, axis=(3, 4), keepdims=True))
        probs = (expos / totals).astype(jnp.bfloat16)
        mixed = jnp.einsum('qhisj,qsjhe->qihe', probs.astype(jnp.float32), values_here)
        return mixed.astype(jnp.bfloat16)
    steps_total = NODE_BLKS // 4
    attended = lax.map(attend, (jnp.arange(NODE_BLKS, dtype=jnp.int32).reshape(steps_total, 4), key_blocks.reshape(steps_total, 4, KB), key_counts.reshape(steps_total, 4)))
    attended = attended.reshape(NODES, D)
    attn_branch = layer_norm(features + jnp.dot(attended, w_out, preferred_element_type=jnp.float32))
    summed = local_branch + attn_branch
    summed_in = summed.astype(jnp.bfloat16)
    activated = jax.nn.gelu(jnp.dot(summed_in, w_up, preferred_element_type=jnp.float32)).astype(jnp.bfloat16)
    layer_out = layer_norm(summed + jnp.dot(activated, w_down, preferred_element_type=jnp.float32))
    return layer_out.astype(jnp.bfloat16)
```

```python
import jax
import jax.numpy as jnp
from jax import lax
from jax.experimental import pallas as pl
from jax.experimental.pallas import tpu as pltpu
from jax.sharding import PartitionSpec as P

MESH = pl.DeviceIdType.MESH
BF = jnp.bfloat16
F32 = jnp.float32
HEADS = 32
HEAD = 32
RING = 4
STEPS = (0, -1, 1, 2)
ONES_LANE = 2 * HEAD


def wrap(v):
    return (v + RING) % RING


def place():
    d = lax.axis_index("dev")
    return d, d // 8, (d // 2) % 4, d % 2


def dev_of(y, z, c):
    return y * 8 + z * 2 + c


def dot(a, b):
    return jnp.dot(a, b, preferred_element_type=F32)


def dot_nt(a, b):
    return lax.dot_general(a, b, (((1,), (1,)), ((), ())), preferred_element_type=F32)


def dot_tn(a, b):
    return lax.dot_general(a, b, (((0,), (0,)), ((), ())), preferred_element_type=F32)


def layer_norm(values):
    average = jnp.mean(values, axis=-1, keepdims=True)
    centered = values - average
    variance = jnp.mean(centered * centered, axis=-1, keepdims=True)
    return centered / jnp.sqrt(variance + 1e-05)


def gather_kernel(
    x_hbm, wg_hbm, wqkv_hbm, inner_ref, outer_ref,
    q_hbm, kv_hbm, tab_hbm,
    xall, idx, wg, w3, wc, xsel, tab, q, kv, outsel,
    send_sem, recv_sem, isend, irecv, sib_send, sib_recv, sibi_send, sibi_recv,
    out_send, out_recv, local_sem, back_sem,
):
    d, y, z, c = place()
    g = lax.axis_index("group")
    sib = dev_of(y, z, 1 - c)
    near = [
        dev_of(wrap(y + 1), z, c), dev_of(wrap(y - 1), z, c),
        dev_of(y, wrap(z + 1), c), dev_of(y, wrap(z - 1), c), sib,
    ]
    bar = pltpu.get_barrier_semaphore()
    for n in near:
        pl.semaphore_signal(bar, inc=1, device_id={"dev": n}, device_id_type=MESH)
    for r in range(1, 4):
        pl.semaphore_signal(bar, inc=1, device_id={"group": wrap(g + r)}, device_id_type=MESH)
    me = y * 4 + z
    loads = [
        pltpu.make_async_copy(x_hbm.at[pl.ds(b * 128, 128)], xall.at[me, c, b], local_sem.at[b])
        for b in range(2)
    ]
    loads.append(pltpu.make_async_copy(wg_hbm, wg, local_sem.at[2]))
    window = pl.multiple_of((d // 4) * 128, 128)
    for t in range(3):
        loads.append(
            pltpu.make_async_copy(
                wqkv_hbm.at[:, pl.ds(t * 1024 + window, 128)], w3.at[t], local_sem.at[3 + t]
            )
        )
    for load in loads:
        load.start()
    idx[me, c, :, 0:64] = inner_ref[0]
    idx[me, c, :, 64:128] = jnp.zeros((32, 64), jnp.int32)
    pl.semaphore_wait(bar, len(near) + 3)
    loads[0].wait()
    loads[1].wait()
    started = []

    class Route:
        def __init__(self, b):
            self.b = b
            self.p, self.s = (y, z) if b == 0 else (z, y)

        def chip(self, dp, ds):
            p, s = wrap(self.p + dp), wrap(self.s + ds)
            return p * 4 + s if self.b == 0 else s * 4 + p

        def target(self, dp, ds):
            p, s = wrap(self.p + dp), wrap(self.s + ds)
            return dev_of(p, s, c) if self.b == 0 else dev_of(s, p, c)

        def view(self, dp, ds, half):
            r = xall.at[self.chip(dp, ds), c, self.b]
            return r if half is None else r.at[pl.ds(half * 64, 64)]

        def copies(self, tag, dp, ds, half, to):
            v = self.view(dp, ds, half)
            k = self.b * 20 + tag
            out = [
                pltpu.make_async_remote_copy(
                    v, v, send_sem.at[k], recv_sem.at[k], device_id={"dev": to}, device_id_type=MESH
                )
            ]
            if self.b == 0 and half != 1:
                v = idx.at[self.chip(dp, ds), c]
                out.append(
                    pltpu.make_async_remote_copy(
                        v, v, isend.at[tag], irecv.at[tag], device_id={"dev": to}, device_id_type=MESH
                    )
                )
            return out

        def send(self, tag, dp, ds, half, to_p, to_s):
            for copy in self.copies(tag, dp, ds, half, self.target(to_p, to_s)):
                copy.start()
                started.append(copy)

        def wait(self, tag, dp, ds, half=None):
            for copy in self.copies(tag, dp, ds, half, sib):
                copy.wait_recv()

        def sib_copy(self, dp, ds):
            i = self.chip(dp, ds)
            v = self.view(dp, ds, None)
            copies = [
                pltpu.make_async_remote_copy(
                    v, v, sib_send.at[i * 2 + self.b], sib_recv.at[i * 2 + self.b],
                    device_id={"dev": sib}, device_id_type=MESH,
                )
            ]
            if self.b == 0:
                v = idx.at[i, c]
                copies.append(
                    pltpu.make_async_remote_copy(
                        v, v, sibi_send.at[i], sibi_recv.at[i],
                        device_id={"dev": sib}, device_id_type=MESH,
                    )
                )
            for copy in copies:
                copy.start()
                started.append(copy)

    def sib_wait(chip):
        for b in range(2):
            v = xall.at[chip, 1 - c, b]
            pltpu.make_async_remote_copy(
                v, v, sib_send.at[chip * 2 + b], sib_recv.at[chip * 2 + b],
                device_id={"dev": sib}, device_id_type=MESH,
            ).wait_recv()
        v = idx.at[chip, 1 - c]
        pltpu.make_async_remote_copy(
            v, v, sibi_send.at[chip], sibi_recv.at[chip],
            device_id={"dev": sib}, device_id_type=MESH,
        ).wait_recv()

    lane = lax.broadcasted_iota(jnp.int32, (256, 128), 1)
    row = lax.broadcasted_iota(jnp.int32, (256, 64), 0)

    def back(k, src, dst):
        return pltpu.make_async_copy(src, dst, back_sem.at[k])

    def backs(chip):
        return [
            back(chip * 3, q.at[pl.ds(chip * 4, 4)], q_hbm.at[pl.ds(chip * 4, 4)]),
            back(chip * 3 + 1, kv.at[pl.ds(chip * 4, 4)], kv_hbm.at[pl.ds(chip * 4, 4)]),
            back(chip * 3 + 2, tab.at[2 + chip], tab_hbm.at[2 + chip]),
        ]

    def process(chip):
        sib_wait(chip)
        for cc in range(2):
            rows = xall[chip, cc].reshape(256, 1024)
            both = dot(rows, wc[...])
            at = chip * 4 + cc * 2
            q[pl.ds(at, 2)] = both[:, :128].astype(BF).reshape(2, 128, 128)
            kv[pl.ds(at, 2)] = (
                jnp.where(lane == ONES_LANE, 1.0, both[:, 128:]).astype(BF).reshape(2, 128, 128)
            )
            picks = idx[chip, cc, pl.ds(d, 1), :][:, 0:64]
            hot = jnp.where(row == picks, 1.0, 0.0).astype(BF)
            xsel[pl.ds(cc * 64, 64), :] = dot_tn(hot, rows).astype(BF)
        tab[2 + chip] = dot(xsel[...], wg[...]).astype(BF)
        for copy in backs(chip):
            copy.start()

    def process_many(count, where):
        def step(i, carry):
            dy, dz = where(i)
            process(wrap(y + dy) * 4 + wrap(z + dz))
            return carry

        lax.fori_loop(0, count, step, 0)

    routes = [Route(0), Route(1)]
    for t in routes:
        t.send(0, 0, 0, None, 1, 0)
        t.send(1, 0, 0, None, -1, 0)
    for t in routes:
        t.send(4, 0, 0, None, 0, 1)
        t.send(5, 0, 0, None, 0, -1)
    for t in routes:
        t.sib_copy(0, 0)

    loads[2].wait()
    own = dot(xall[me, c].reshape(256, 1024), wg[...]).astype(BF)
    tab[0:2] = own.reshape(2, 128, 1024)
    for r in range(4):
        to = wrap(g + r)
        picks = outer_ref[0, pl.ds(to, 1), :]
        hot = jnp.where(
            lax.broadcasted_iota(jnp.int32, (256, 128), 0) == picks, 1.0, 0.0
        ).astype(BF)
        rows = dot_tn(hot, own).astype(BF)
        if r == 0:
            tab[18 + g] = rows
        else:
            outsel[r - 1] = rows
            copy = pltpu.make_async_remote_copy(
                outsel.at[r - 1], tab.at[18 + g], out_send.at[r - 1], out_recv.at[r - 1],
                device_id={"group": to}, device_id_type=MESH,
            )
            copy.start()
            started.append(copy)

    for t in range(3):
        loads[3 + t].wait()
    take = lax.broadcasted_iota(jnp.int32, (128, 256), 0) - (d % 4) * HEAD
    col = lax.broadcasted_iota(jnp.int32, (128, 256), 1)
    total = jnp.zeros((1024, 256), F32)
    for t in range(3):
        first = (0, 128, 128 + HEAD)[t]
        inside = (take >= 0) & (take < HEAD) & (col == take + first)
        total = total + dot(w3[t], jnp.where(inside, 1.0, 0.0).astype(BF))
    wc[...] = total.astype(BF)

    def e1():
        for t in routes:
            t.wait(0, -1, 0)
            t.send(2, -1, 0, 0, 1, 0)
            t.wait(1, 1, 0)
            t.send(3, 1, 0, 1, -1, 0)
        for t in routes:
            for k in (1, 2):
                t.send(4 + 4 * k, STEPS[k], 0, None, 0, 1)
                t.send(5 + 4 * k, STEPS[k], 0, None, 0, -1)
                t.sib_copy(STEPS[k], 0)

    def e2():
        for t in routes:
            t.wait(2, 2, 0, 0)
            t.wait(3, 2, 0, 1)
            t.send(16, 2, 0, None, 0, 1)
            t.send(17, 2, 0, None, 0, -1)
            t.sib_copy(2, 0)

    def e3(k):
        for t in routes:
            t.wait(4 + 4 * k, STEPS[k], -1)
            t.send(6 + 4 * k, STEPS[k], -1, 0, 0, 1)
            t.wait(5 + 4 * k, STEPS[k], 1)
            t.send(7 + 4 * k, STEPS[k], 1, 1, 0, -1)
            t.sib_copy(STEPS[k], -1)
            t.sib_copy(STEPS[k], 1)

    def e4(k):
        for t in routes:
            t.wait(6 + 4 * k, STEPS[k], 2, 0)
            t.wait(7 + 4 * k, STEPS[k], 2, 1)
            t.sib_copy(STEPS[k], 2)

    def sign(i):
        return 1 - 2 * (i % 2)

    e1()
    process_many(1, lambda i: (0 * i, 0 * i))
    e2()
    e3(0)
    process_many(2, lambda i: (sign(i), 0 * i))
    e3(1)
    e4(0)
    process_many(
        4,
        lambda i: (
            (i // 2) * 2 * (i % 2),
            sign(i) * (1 - i // 2) + (i // 2) * 2 * (1 - i % 2),
        ),
    )
    e3(2)
    e4(1)
    process_many(4, lambda i: (sign(i), 1 - 2 * (i // 2)))
    e3(3)
    e4(2)
    process_many(
        4,
        lambda i: (
            sign(i) * (1 - i // 2) + 2 * (i // 2),
            sign(i) * (i // 2) + 2 * (1 - i // 2),
        ),
    )
    e4(3)
    process_many(1, lambda i: (2 + 0 * i, 2 + 0 * i))

    for r in range(1, 4):
        pltpu.make_async_remote_copy(
            outsel.at[r - 1], tab.at[18 + wrap(g - r)], out_send.at[r - 1], out_recv.at[r - 1],
            device_id={"group": wrap(g + r)}, device_id_type=MESH,
        ).wait_recv()
    kv[64] = jnp.zeros((128, 128), BF)
    tails = [
        back(48, tab.at[pl.ds(0, 2)], tab_hbm.at[pl.ds(0, 2)]),
        back(49, tab.at[pl.ds(18, 4)], tab_hbm.at[pl.ds(18, 4)]),
        back(50, kv.at[64], kv_hbm.at[64]),
    ]
    for copy in tails:
        copy.start()
    for copy in started:
        copy.wait_send()
    for chip in range(16):
        for copy in backs(chip):
            copy.wait()
    for copy in tails:
        copy.wait()


def attend_kernel(blocks, counts, q_ref, kv_ref, o_ref, s_ref):
    factor = 1.4426950408889634 / HEAD**0.5
    dead = kv_ref.shape[0] - 1

    def one(i, lanes, slots):
        query = q_ref[i]
        count = counts[i]
        first = blocks[i, 0]
        highest = None
        for s in range(slots):
            at = jnp.where(s < count, blocks[i, s], first)
            scores = dot_nt(query, kv_ref[at])
            s_ref[s] = scores
            highest = scores if highest is None else jnp.maximum(highest, scores)
        top = jnp.max(highest, axis=1, keepdims=True) * factor
        mixed = None
        for s in range(slots):
            at = jnp.where(s < count, blocks[i, s], dead)
            probs = jnp.exp2(s_ref[s] * factor - top).astype(BF)
            part = dot(probs, kv_ref[at])
            mixed = part if mixed is None else mixed + part
        turned = mixed.T
        part = turned[HEAD : 2 * HEAD] / turned[ONES_LANE : ONES_LANE + 1]
        o_ref[i // 2, :, lanes * 128 : lanes * 128 + 128] = part.astype(BF)

    def step(j, carry):
        for lanes in range(2):
            i = 2 * j + lanes
            fours = (counts[i] + 3) // 4
            for n in range(1, 5):
                @pl.when(fours == n)
                def _():
                    one(i, lanes, 4 * n)
        return carry

    lax.fori_loop(0, q_ref.shape[0] // 2, step, 0)


def finish_kernel(
    ot, tab_hbm, adj_hbm, nb_ref, x_ref, wo_hbm, wu_hbm, wd_hbm,
    o_ref,
    ret, tab, adj, wo, wu, wd, summed,
    send_sem, recv_sem, local_sem,
):
    d, y, z, c = place()
    loads = [
        pltpu.make_async_copy(src, dst, local_sem.at[i])
        for i, (src, dst) in enumerate(
            ((adj_hbm, adj), (tab_hbm, tab), (wo_hbm, wo), (wu_hbm, wu), (wd_hbm, wd), (ot.at[d], ret.at[d]))
        )
    ]
    bar = pltpu.get_barrier_semaphore()

    def other(r):
        return dev_of(wrap(y + r // 8), wrap(z + (r // 2) % 4), (c + r % 2) % 2)

    def source(r):
        return dev_of(wrap(y - r // 8), wrap(z - (r // 2) % 4), (c + r % 2) % 2)

    def hail(r, carry):
        pl.semaphore_signal(bar, inc=1, device_id={"dev": other(r)}, device_id_type=MESH)
        return carry

    lax.fori_loop(1, 32, hail, 0)
    for load in loads:
        load.start()
    pl.semaphore_wait(bar, 31)

    def copy(r):
        return pltpu.make_async_remote_copy(
            ot.at[other(r)], ret.at[d], send_sem.at[r], recv_sem.at[r],
            device_id={"dev": other(r)}, device_id_type=MESH,
        )

    def arrive(r):
        return pltpu.make_async_remote_copy(
            ot.at[other(r)], ret.at[source(r)], send_sem.at[r], recv_sem.at[r],
            device_id={"dev": other(r)}, device_id_type=MESH,
        )

    def push(r, carry):
        copy(r).start()
        return carry

    lax.fori_loop(1, 32, push, 0)
    loads[0].wait()
    loads[1].wait()
    for b in range(2):
        total = None
        for s in range(16):
            part = dot(adj[b, s], tab[nb_ref[b, s]])
            total = part if total is None else total + part
        features = x_ref[pl.ds(b * 128, 128), :].astype(F32)
        summed[pl.ds(b * 128, 128), :] = layer_norm(features + total)
    loads[2].wait()
    loads[5].wait()

    def land(r, carry):
        arrive(r).wait_recv()
        return carry

    lax.fori_loop(1, 32, land, 0)
    projected = dot_tn(ret[...].reshape(1024, 256), wo[...])
    both = summed[...] + layer_norm(x_ref[...].astype(F32) + projected)
    summed[...] = both
    loads[3].wait()
    hidden = jax.nn.gelu(dot(both.astype(BF), wu[...])).astype(BF)
    loads[4].wait()
    o_ref[...] = layer_norm(summed[...] + dot(hidden, wd[...])).astype(BF)

    def leave(r, carry):
        copy(r).wait_send()
        return carry

    lax.fori_loop(1, 32, leave, 0)


def per_device(
    node_feats, w_gcn, adj_tiles, neighbor_blocks, inner_rows, outer_rows,
    w_qkv, key_blocks, key_counts, w_out, w_up, w_down,
):
    hbm = pl.BlockSpec(memory_space=pl.ANY)
    vmem = pl.BlockSpec(memory_space=pltpu.VMEM)
    smem = pl.BlockSpec(memory_space=pltpu.SMEM)
    dma = pltpu.SemaphoreType.DMA
    q, kv, tab = pl.pallas_call(
        gather_kernel,
        out_shape=(
            jax.ShapeDtypeStruct((64, 128, 128), BF),
            jax.ShapeDtypeStruct((65, 128, 128), BF),
            jax.ShapeDtypeStruct((22, 128, 1024), BF),
        ),
        in_specs=[hbm, hbm, hbm, vmem, vmem],
        out_specs=(hbm, hbm, hbm),
        scratch_shapes=[
            pltpu.VMEM((16, 2, 2, 128, 1024), BF),
            pltpu.VMEM((16, 2, 32, 128), jnp.int32),
            pltpu.VMEM((1024, 1024), BF),
            pltpu.VMEM((3, 1024, 128), BF),
            pltpu.VMEM((1024, 256), BF),
            pltpu.VMEM((128, 1024), BF),
            pltpu.VMEM((22, 128, 1024), BF),
            pltpu.VMEM((64, 128, 128), BF),
            pltpu.VMEM((65, 128, 128), BF),
            pltpu.VMEM((3, 128, 1024), BF),
            dma((40,)), dma((40,)), dma((20,)), dma((20,)), dma((32,)), dma((32,)), dma((16,)), dma((16,)),
            dma((3,)), dma((3,)), dma((6,)), dma((51,)),
        ],
        compiler_params=pltpu.CompilerParams(
            collective_id=0, has_side_effects=True, vmem_limit_bytes=48 << 20
        ),
        name="gather",
    )(node_feats, w_gcn, w_qkv, inner_rows, outer_rows)
    ot = pl.pallas_call(
        attend_kernel,
        out_shape=jax.ShapeDtypeStruct((32, 32, 256), BF),
        in_specs=[smem, smem, vmem, vmem],
        out_specs=vmem,
        scratch_shapes=[pltpu.VMEM((16, 128, 128), F32)],
        compiler_params=pltpu.CompilerParams(vmem_limit_bytes=32 << 20),
        name="attend",
    )(key_blocks, key_counts, q, kv)
    return pl.pallas_call(
        finish_kernel,
        out_shape=jax.ShapeDtypeStruct((256, 1024), BF),
        in_specs=[hbm, hbm, hbm, smem, vmem, hbm, hbm, hbm],
        out_specs=vmem,
        scratch_shapes=[
            pltpu.VMEM((32, 32, 256), BF),
            pltpu.VMEM((22, 128, 1024), BF),
            pltpu.VMEM((2, 16, 128, 128), BF),
            pltpu.VMEM((1024, 1024), BF),
            pltpu.VMEM((1024, 2048), BF),
            pltpu.VMEM((2048, 1024), BF),
            pltpu.VMEM((256, 1024), F32),
            dma((32,)), dma((32,)), dma((6,)),
        ],
        compiler_params=pltpu.CompilerParams(
            collective_id=1, has_side_effects=True, vmem_limit_bytes=48 << 20
        ),
        name="finish",
    )(ot, tab, adj_tiles, neighbor_blocks, node_feats, w_out, w_up, w_down)


def solution(mesh):
    placed = (
        P(("group", "dev"), None),
        P(),
        P(("group", "dev"), None, None, None),
        P(("group", "dev"), None),
        P(("group", "dev"), None, None),
        P(("group", "dev"), None, None),
        P(),
        P("group", None),
        P("group"),
        P(),
        P(),
        P(),
    )
    return jax.shard_map(
        per_device, mesh=mesh, in_specs=placed, out_specs=P(("group", "dev"), None), check_vma=False
    )
```

```python
import jax
import jax.numpy as jnp
from jax import lax
from jax.experimental import pallas as pl
from jax.experimental.pallas import tpu as pltpu
from jax.sharding import PartitionSpec as P

MESH = pl.DeviceIdType.MESH
BF = jnp.bfloat16
F32 = jnp.float32
HEADS = 32
HEAD = 32
RING = 4
STEPS = (0, -1, 1, 2)
ONES_LANE = 2 * HEAD


def wrap(v):
    return (v + RING) % RING


def place():
    d = lax.axis_index("dev")
    return d, d // 8, (d // 2) % 4, d % 2


def dev_of(y, z, c):
    return y * 8 + z * 2 + c


def dot(a, b):
    return jnp.dot(a, b, preferred_element_type=F32)


def dot_nt(a, b):
    return lax.dot_general(a, b, (((1,), (1,)), ((), ())), preferred_element_type=F32)


def dot_tn(a, b):
    return lax.dot_general(a, b, (((0,), (0,)), ((), ())), preferred_element_type=F32)


def layer_norm(values):
    average = jnp.mean(values, axis=-1, keepdims=True)
    centered = values - average
    variance = jnp.mean(centered * centered, axis=-1, keepdims=True)
    return centered / jnp.sqrt(variance + 1e-05)


def gather_kernel(
    x_hbm, wg_hbm, wqkv_hbm, inner_ref, outer_ref,
    q_hbm, kv_hbm, tab_hbm,
    xall, idx, wg, w3, wc, xsel, tab, q, kv, outsel,
    send_sem, recv_sem, isend, irecv, sib_send, sib_recv, sibi_send, sibi_recv,
    out_send, out_recv, local_sem, back_sem,
):
    d, y, z, c = place()
    g = lax.axis_index("group")
    sib = dev_of(y, z, 1 - c)
    near = [
        dev_of(wrap(y + 1), z, c), dev_of(wrap(y - 1), z, c),
        dev_of(y, wrap(z + 1), c), dev_of(y, wrap(z - 1), c), sib,
    ]
    bar = pltpu.get_barrier_semaphore()
    for n in near:
        pl.semaphore_signal(bar, inc=1, device_id={"dev": n}, device_id_type=MESH)
    for r in range(1, 4):
        pl.semaphore_signal(bar, inc=1, device_id={"group": wrap(g + r)}, device_id_type=MESH)
    me = y * 4 + z
    loads = [
        pltpu.make_async_copy(x_hbm.at[pl.ds(b * 128, 128)], xall.at[me, c, b], local_sem.at[b])
        for b in range(2)
    ]
    loads.append(pltpu.make_async_copy(wg_hbm, wg, local_sem.at[2]))
    window = pl.multiple_of((d // 4) * 128, 128)
    for t in range(3):
        loads.append(
            pltpu.make_async_copy(
                wqkv_hbm.at[:, pl.ds(t * 1024 + window, 128)], w3.at[t], local_sem.at[3 + t]
            )
        )
    for load in loads:
        load.start()
    idx[me, c, :, 0:64] = inner_ref[0]
    idx[me, c, :, 64:128] = jnp.zeros((32, 64), jnp.int32)
    pl.semaphore_wait(bar, len(near) + 3)
    loads[0].wait()
    loads[1].wait()
    started = []

    class Route:
        def __init__(self, b):
            self.b = b
            self.p, self.s = (y, z) if b == 0 else (z, y)

        def chip(self, dp, ds):
            p, s = wrap(self.p + dp), wrap(self.s + ds)
            return p * 4 + s if self.b == 0 else s * 4 + p

        def target(self, dp, ds):
            p, s = wrap(self.p + dp), wrap(self.s + ds)
            return dev_of(p, s, c) if self.b == 0 else dev_of(s, p, c)

        def view(self, dp, ds, half):
            r = xall.at[self.chip(dp, ds), c, self.b]
            return r if half is None else r.at[pl.ds(half * 64, 64)]

        def copies(self, tag, dp, ds, half, to):
            v = self.view(dp, ds, half)
            k = self.b * 20 + tag
            out = [
                pltpu.make_async_remote_copy(
                    v, v, send_sem.at[k], recv_sem.at[k], device_id={"dev": to}, device_id_type=MESH
                )
            ]
            if self.b == 0 and half != 1:
                v = idx.at[self.chip(dp, ds), c]
                out.append(
                    pltpu.make_async_remote_copy(
                        v, v, isend.at[tag], irecv.at[tag], device_id={"dev": to}, device_id_type=MESH
                    )
                )
            return out

        def send(self, tag, dp, ds, half, to_p, to_s):
            for copy in self.copies(tag, dp, ds, half, self.target(to_p, to_s)):
                copy.start()
                started.append(copy)

        def wait(self, tag, dp, ds, half=None):
            for copy in self.copies(tag, dp, ds, half, sib):
                copy.wait_recv()

        def sib_copy(self, dp, ds):
            i = self.chip(dp, ds)
            v = self.view(dp, ds, None)
            copies = [
                pltpu.make_async_remote_copy(
                    v, v, sib_send.at[i * 2 + self.b], sib_recv.at[i * 2 + self.b],
                    device_id={"dev": sib}, device_id_type=MESH,
                )
            ]
            if self.b == 0:
                v = idx.at[i, c]
                copies.append(
                    pltpu.make_async_remote_copy(
                        v, v, sibi_send.at[i], sibi_recv.at[i],
                        device_id={"dev": sib}, device_id_type=MESH,
                    )
                )
            for copy in copies:
                copy.start()
                started.append(copy)

    def sib_wait(chip):
        for b in range(2):
            v = xall.at[chip, 1 - c, b]
            pltpu.make_async_remote_copy(
                v, v, sib_send.at[chip * 2 + b], sib_recv.at[chip * 2 + b],
                device_id={"dev": sib}, device_id_type=MESH,
            ).wait_recv()
        v = idx.at[chip, 1 - c]
        pltpu.make_async_remote_copy(
            v, v, sibi_send.at[chip], sibi_recv.at[chip],
            device_id={"dev": sib}, device_id_type=MESH,
        ).wait_recv()

    lane = lax.broadcasted_iota(jnp.int32, (256, 128), 1)
    row = lax.broadcasted_iota(jnp.int32, (256, 64), 0)

    def back(k, src, dst):
        return pltpu.make_async_copy(src, dst, back_sem.at[k])

    def backs(chip):
        return [
            back(chip * 3, q.at[pl.ds(chip * 4, 4)], q_hbm.at[pl.ds(chip * 4, 4)]),
            back(chip * 3 + 1, kv.at[pl.ds(chip * 4, 4)], kv_hbm.at[pl.ds(chip * 4, 4)]),
            back(chip * 3 + 2, tab.at[2 + chip], tab_hbm.at[2 + chip]),
        ]

    def process(chip):
        sib_wait(chip)
        for cc in range(2):
            rows = xall[chip, cc].reshape(256, 1024)
            both = dot(rows, wc[...])
            at = chip * 4 + cc * 2
            q[pl.ds(at, 2)] = both[:, :128].astype(BF).reshape(2, 128, 128)
            kv[pl.ds(at, 2)] = (
                jnp.where(lane == ONES_LANE, 1.0, both[:, 128:]).astype(BF).reshape(2, 128, 128)
            )
            picks = idx[chip, cc, pl.ds(d, 1), :][:, 0:64]
            hot = jnp.where(row == picks, 1.0, 0.0).astype(BF)
            xsel[pl.ds(cc * 64, 64), :] = dot_tn(hot, rows).astype(BF)
        tab[2 + chip] = dot(xsel[...], wg[...]).astype(BF)
        for copy in backs(chip):
            copy.start()

    def process_many(count, where):
        def step(i, carry):
            dy, dz = where(i)
            process(wrap(y + dy) * 4 + wrap(z + dz))
            return carry

        lax.fori_loop(0, count, step, 0)

    routes = [Route(0), Route(1)]
    for t in routes:
        t.send(0, 0, 0, None, 1, 0)
        t.send(1, 0, 0, None, -1, 0)
    for t in routes:
        t.send(4, 0, 0, None, 0, 1)
        t.send(5, 0, 0, None, 0, -1)
    for t in routes:
        t.sib_copy(0, 0)

    loads[2].wait()
    own = dot(xall[me, c].reshape(256, 1024), wg[...]).astype(BF)
    tab[0:2] = own.reshape(2, 128, 1024)
    for r in range(4):
        to = wrap(g + r)
        picks = outer_ref[0, pl.ds(to, 1), :]
        hot = jnp.where(
            lax.broadcasted_iota(jnp.int32, (256, 128), 0) == picks, 1.0, 0.0
        ).astype(BF)
        rows = dot_tn(hot, own).astype(BF)
        if r == 0:
            tab[18 + g] = rows
        else:
            outsel[r - 1] = rows
            copy = pltpu.make_async_remote_copy(
                outsel.at[r - 1], tab.at[18 + g], out_send.at[r - 1], out_recv.at[r - 1],
                device_id={"group": to}, device_id_type=MESH,
            )
            copy.start()
            started.append(copy)

    for t in range(3):
        loads[3 + t].wait()
    take = lax.broadcasted_iota(jnp.int32, (128, 256), 0) - (d % 4) * HEAD
    col = lax.broadcasted_iota(jnp.int32, (128, 256), 1)
    total = jnp.zeros((1024, 256), F32)
    for t in range(3):
        first = (0, 128, 128 + HEAD)[t]
        inside = (take >= 0) & (take < HEAD) & (col == take + first)
        total = total + dot(w3[t], jnp.where(inside, 1.0, 0.0).astype(BF))
    wc[...] = total.astype(BF)

    def e1():
        for t in routes:
            t.wait(0, -1, 0)
            t.send(2, -1, 0, 0, 1, 0)
            t.wait(1, 1, 0)
            t.send(3, 1, 0, 1, -1, 0)
        for t in routes:
            for k in (1, 2):
                t.send(4 + 4 * k, STEPS[k], 0, None, 0, 1)
                t.send(5 + 4 * k, STEPS[k], 0, None, 0, -1)
                t.sib_copy(STEPS[k], 0)

    def e2():
        for t in routes:
            t.wait(2, 2, 0, 0)
            t.wait(3, 2, 0, 1)
            t.send(16, 2, 0, None, 0, 1)
            t.send(17, 2, 0, None, 0, -1)
            t.sib_copy(2, 0)

    def e3(k):
        for t in routes:
            t.wait(4 + 4 * k, STEPS[k], -1)
            t.send(6 + 4 * k, STEPS[k], -1, 0, 0, 1)
            t.wait(5 + 4 * k, STEPS[k], 1)
            t.send(7 + 4 * k, STEPS[k], 1, 1, 0, -1)
            t.sib_copy(STEPS[k], -1)
            t.sib_copy(STEPS[k], 1)

    def e4(k):
        for t in routes:
            t.wait(6 + 4 * k, STEPS[k], 2, 0)
            t.wait(7 + 4 * k, STEPS[k], 2, 1)
            t.sib_copy(STEPS[k], 2)

    def sign(i):
        return 1 - 2 * (i % 2)

    e1()
    process_many(1, lambda i: (0 * i, 0 * i))
    e2()
    e3(0)
    process_many(2, lambda i: (sign(i), 0 * i))
    e3(1)
    e4(0)
    process_many(
        4,
        lambda i: (
            (i // 2) * 2 * (i % 2),
            sign(i) * (1 - i // 2) + (i // 2) * 2 * (1 - i % 2),
        ),
    )
    e3(2)
    e4(1)
    process_many(4, lambda i: (sign(i), 1 - 2 * (i // 2)))
    e3(3)
    e4(2)
    process_many(
        4,
        lambda i: (
            sign(i) * (1 - i // 2) + 2 * (i // 2),
            sign(i) * (i // 2) + 2 * (1 - i // 2),
        ),
    )
    e4(3)
    process_many(1, lambda i: (2 + 0 * i, 2 + 0 * i))

    for r in range(1, 4):
        pltpu.make_async_remote_copy(
            outsel.at[r - 1], tab.at[18 + wrap(g - r)], out_send.at[r - 1], out_recv.at[r - 1],
            device_id={"group": wrap(g + r)}, device_id_type=MESH,
        ).wait_recv()
    kv[64] = jnp.zeros((128, 128), BF)
    tails = [
        back(48, tab.at[pl.ds(0, 2)], tab_hbm.at[pl.ds(0, 2)]),
        back(49, tab.at[pl.ds(18, 4)], tab_hbm.at[pl.ds(18, 4)]),
        back(50, kv.at[64], kv_hbm.at[64]),
    ]
    for copy in tails:
        copy.start()
    for copy in started:
        copy.wait_send()
    for chip in range(16):
        for copy in backs(chip):
            copy.wait()
    for copy in tails:
        copy.wait()


def attend_kernel(blocks, counts, q_ref, kv_ref, o_ref, s_a, s_b, m_a, m_b, order):
    factor = 1.4426950408889634 / HEAD**0.5
    dead = kv_ref.shape[0] - 1
    total = q_ref.shape[0]

    def tally(i, have):
        fours = (counts[i] + 3) // 4
        return tuple(h + jnp.where(fours == n + 1, 1, 0) for n, h in enumerate(have))

    have = lax.fori_loop(0, total, tally, (jnp.int32(0),) * 4)
    first = (jnp.int32(0), have[0], have[0] + have[1], have[0] + have[1] + have[2])

    def enlist(i, at):
        fours = (counts[i] + 3) // 4
        where = at[3]
        for n in range(3):
            where = jnp.where(fours == n + 1, at[n], where)
        order[where] = i
        return tuple(a + jnp.where(fours == n + 1, 1, 0) for n, a in enumerate(at))

    lax.fori_loop(0, total, enlist, first)

    def score(i, slots, scores, tops):
        query = q_ref[i]
        highest = None
        for s in range(0, slots, 2):
            keys = [
                kv_ref[jnp.where(s + u < counts[i], blocks[i, s + u], blocks[i, 0])] for u in range(2)
            ]
            part = dot_nt(query, jnp.concatenate(keys, axis=0))
            scores[:, pl.ds(s * 128, 256)] = part
            part = jnp.maximum(part[:, :128], part[:, 128:])
            highest = part if highest is None else jnp.maximum(highest, part)
        tops[...] = jnp.broadcast_to(jnp.max(highest, axis=1, keepdims=True) * factor, (128, 128))

    def mix(i, slots, scores, tops):
        top = jnp.concatenate([tops[...]] * 2, axis=1)
        mixed = None
        for s in range(0, slots, 2):
            probs = jnp.exp2(scores[:, pl.ds(s * 128, 256)] * factor - top).astype(BF)
            values = [
                kv_ref[jnp.where(s + u < counts[i], blocks[i, s + u], dead)] for u in range(2)
            ]
            part = dot(probs, jnp.concatenate(values, axis=0))
            mixed = part if mixed is None else mixed + part
        turned = mixed.T
        part = turned[HEAD : 2 * HEAD] / turned[ONES_LANE : ONES_LANE + 1]
        o_ref[i // 2, :, pl.ds(pl.multiple_of((i % 2) * 128, 128), 128)] = part.astype(BF)

    for n in range(4):
        slots = 4 * n + 4
        count, start = have[n], first[n]

        def item(t):
            return order[start + jnp.minimum(t, count - 1)]

        @pl.when(count > 0)
        def _():
            score(item(0), slots, s_a, m_a)

            def step(t, carry):
                score(item(2 * t + 1), slots, s_b, m_b)
                mix(item(2 * t), slots, s_a, m_a)
                score(item(2 * t + 2), slots, s_a, m_a)
                mix(item(2 * t + 1), slots, s_b, m_b)
                return carry

            lax.fori_loop(0, (count + 1) // 2, step, 0)


def finish_kernel(
    ot, tab_hbm, adj_hbm, nb_ref, x_ref, wo_hbm, wu_hbm, wd_hbm,
    o_ref,
    ret, tab, adj, wo, wu, wd, summed,
    send_sem, recv_sem, local_sem,
):
    d, y, z, c = place()
    loads = [
        pltpu.make_async_copy(src, dst, local_sem.at[i])
        for i, (src, dst) in enumerate(
            ((adj_hbm, adj), (tab_hbm, tab), (wo_hbm, wo), (wu_hbm, wu), (wd_hbm, wd), (ot.at[d], ret.at[d]))
        )
    ]
    bar = pltpu.get_barrier_semaphore()

    def other(r):
        return dev_of(wrap(y + r // 8), wrap(z + (r // 2) % 4), (c + r % 2) % 2)

    def source(r):
        return dev_of(wrap(y - r // 8), wrap(z - (r // 2) % 4), (c + r % 2) % 2)

    def hail(r, carry):
        pl.semaphore_signal(bar, inc=1, device_id={"dev": other(r)}, device_id_type=MESH)
        return carry

    lax.fori_loop(1, 32, hail, 0)
    for load in loads:
        load.start()
    pl.semaphore_wait(bar, 31)

    def copy(r):
        return pltpu.make_async_remote_copy(
            ot.at[other(r)], ret.at[d], send_sem.at[r], recv_sem.at[r],
            device_id={"dev": other(r)}, device_id_type=MESH,
        )

    def arrive(r):
        return pltpu.make_async_remote_copy(
            ot.at[other(r)], ret.at[source(r)], send_sem.at[r], recv_sem.at[r],
            device_id={"dev": other(r)}, device_id_type=MESH,
        )

    def push(r, carry):
        copy(r).start()
        return carry

    lax.fori_loop(1, 32, push, 0)
    loads[0].wait()
    loads[1].wait()
    for b in range(2):
        total = None
        for s in range(16):
            part = dot(adj[b, s], tab[nb_ref[b, s]])
            total = part if total is None else total + part
        features = x_ref[pl.ds(b * 128, 128), :].astype(F32)
        summed[pl.ds(b * 128, 128), :] = layer_norm(features + total)
    loads[2].wait()
    loads[5].wait()

    def land(r, carry):
        arrive(r).wait_recv()
        return carry

    lax.fori_loop(1, 32, land, 0)
    projected = dot_tn(ret[...].reshape(1024, 256), wo[...])
    both = summed[...] + layer_norm(x_ref[...].astype(F32) + projected)
    summed[...] = both
    loads[3].wait()
    hidden = jax.nn.gelu(dot(both.astype(BF), wu[...])).astype(BF)
    loads[4].wait()
    o_ref[...] = layer_norm(summed[...] + dot(hidden, wd[...])).astype(BF)

    def leave(r, carry):
        copy(r).wait_send()
        return carry

    lax.fori_loop(1, 32, leave, 0)


def per_device(
    node_feats, w_gcn, adj_tiles, neighbor_blocks, inner_rows, outer_rows,
    w_qkv, key_blocks, key_counts, w_out, w_up, w_down,
):
    hbm = pl.BlockSpec(memory_space=pl.ANY)
    vmem = pl.BlockSpec(memory_space=pltpu.VMEM)
    smem = pl.BlockSpec(memory_space=pltpu.SMEM)
    dma = pltpu.SemaphoreType.DMA
    q, kv, tab = pl.pallas_call(
        gather_kernel,
        out_shape=(
            jax.ShapeDtypeStruct((64, 128, 128), BF),
            jax.ShapeDtypeStruct((65, 128, 128), BF),
            jax.ShapeDtypeStruct((22, 128, 1024), BF),
        ),
        in_specs=[hbm, hbm, hbm, vmem, vmem],
        out_specs=(hbm, hbm, hbm),
        scratch_shapes=[
            pltpu.VMEM((16, 2, 2, 128, 1024), BF),
            pltpu.VMEM((16, 2, 32, 128), jnp.int32),
            pltpu.VMEM((1024, 1024), BF),
            pltpu.VMEM((3, 1024, 128), BF),
            pltpu.VMEM((1024, 256), BF),
            pltpu.VMEM((128, 1024), BF),
            pltpu.VMEM((22, 128, 1024), BF),
            pltpu.VMEM((64, 128, 128), BF),
            pltpu.VMEM((65, 128, 128), BF),
            pltpu.VMEM((3, 128, 1024), BF),
            dma((40,)), dma((40,)), dma((20,)), dma((20,)), dma((32,)), dma((32,)), dma((16,)), dma((16,)),
            dma((3,)), dma((3,)), dma((6,)), dma((51,)),
        ],
        compiler_params=pltpu.CompilerParams(
            collective_id=0, has_side_effects=True, vmem_limit_bytes=58 << 20
        ),
        name="gather",
    )(node_feats, w_gcn, w_qkv, inner_rows, outer_rows)
    ot = pl.pallas_call(
        attend_kernel,
        out_shape=jax.ShapeDtypeStruct((32, 32, 256), BF),
        in_specs=[smem, smem, vmem, vmem],
        out_specs=vmem,
        scratch_shapes=[
            pltpu.VMEM((128, 2048), F32),
            pltpu.VMEM((128, 2048), F32),
            pltpu.VMEM((128, 128), F32),
            pltpu.VMEM((128, 128), F32),
            pltpu.SMEM((64,), jnp.int32),
        ],
        compiler_params=pltpu.CompilerParams(vmem_limit_bytes=32 << 20),
        name="attend",
    )(key_blocks, key_counts, q, kv)
    return pl.pallas_call(
        finish_kernel,
        out_shape=jax.ShapeDtypeStruct((256, 1024), BF),
        in_specs=[hbm, hbm, hbm, smem, vmem, hbm, hbm, hbm],
        out_specs=vmem,
        scratch_shapes=[
            pltpu.VMEM((32, 32, 256), BF),
            pltpu.VMEM((22, 128, 1024), BF),
            pltpu.VMEM((2, 16, 128, 128), BF),
            pltpu.VMEM((1024, 1024), BF),
            pltpu.VMEM((1024, 2048), BF),
            pltpu.VMEM((2048, 1024), BF),
            pltpu.VMEM((256, 1024), F32),
            dma((32,)), dma((32,)), dma((6,)),
        ],
        compiler_params=pltpu.CompilerParams(
            collective_id=1, has_side_effects=True, vmem_limit_bytes=58 << 20
        ),
        name="finish",
    )(ot, tab, adj_tiles, neighbor_blocks, node_feats, w_out, w_up, w_down)


def solution(mesh):
    placed = (
        P(("group", "dev"), None),
        P(),
        P(("group", "dev"), None, None, None),
        P(("group", "dev"), None),
        P(("group", "dev"), None, None),
        P(("group", "dev"), None, None),
        P(),
        P("group", None),
        P("group"),
        P(),
        P(),
        P(),
    )
    return jax.shard_map(
        per_device, mesh=mesh, in_specs=placed, out_specs=P(("group", "dev"), None), check_vma=False
    )
```

```python
import jax
import jax.numpy as jnp
from jax import lax
from jax.experimental import pallas as pl
from jax.experimental.pallas import tpu as pltpu
from jax.sharding import PartitionSpec as P

MESH = pl.DeviceIdType.MESH
BF = jnp.bfloat16
F32 = jnp.float32
HEADS = 32
HEAD = 32
RING = 4
STEPS = (0, -1, 1, 2)
ONES_LANE = 2 * HEAD


def wrap(v):
    return (v + RING) % RING


def place():
    d = lax.axis_index("dev")
    return d, d // 8, (d // 2) % 4, d % 2


def dev_of(y, z, c):
    return y * 8 + z * 2 + c


def dot(a, b):
    return jnp.dot(a, b, preferred_element_type=F32)


def dot_nt(a, b):
    return lax.dot_general(a, b, (((1,), (1,)), ((), ())), preferred_element_type=F32)


def dot_tn(a, b):
    return lax.dot_general(a, b, (((0,), (0,)), ((), ())), preferred_element_type=F32)


def layer_norm(values):
    average = jnp.mean(values, axis=-1, keepdims=True)
    centered = values - average
    variance = jnp.mean(centered * centered, axis=-1, keepdims=True)
    return centered / jnp.sqrt(variance + 1e-05)


def layer_kernel(
    x_hbm, wg_hbm, wqkv_hbm, inner_hbm, outer_hbm, adj_hbm, nb_hbm, blocks_hbm, counts_hbm,
    wo_hbm, wu_hbm, wd_hbm,
    o_ref,
    xall, idx, wg, w3, wc, xsel, q, kv, outsel, outin, inner_ref, outer_ref, adj, acc,
    wo, wu, wd, ob, ret, s_a, s_b, m_a, m_b, nb, blocks, counts,
    send_sem, recv_sem, isend, irecv, sib_send, sib_recv, sibi_send, sibi_recv,
    out_send, out_recv, local_sem, ret_send, ret_recv,
):
    d, y, z, c = place()
    g = lax.axis_index("group")
    sib = dev_of(y, z, 1 - c)
    bar = pltpu.get_barrier_semaphore()

    def other(r):
        return dev_of(wrap(y + r // 8), wrap(z + (r // 2) % 4), (c + r % 2) % 2)

    def source(r):
        return dev_of(wrap(y - r // 8), wrap(z - (r // 2) % 4), (c + r % 2) % 2)

    def hail(r, carry):
        pl.semaphore_signal(bar, inc=1, device_id={"dev": other(r)}, device_id_type=MESH)
        return carry

    lax.fori_loop(1, 32, hail, 0)
    for r in range(1, 4):
        pl.semaphore_signal(bar, inc=1, device_id={"group": wrap(g + r)}, device_id_type=MESH)
    me = y * 4 + z
    loads = [
        pltpu.make_async_copy(x_hbm.at[pl.ds(b * 128, 128)], xall.at[me, c, b], local_sem.at[b])
        for b in range(2)
    ]
    loads.append(pltpu.make_async_copy(wg_hbm, wg, local_sem.at[2]))
    window = pl.multiple_of((d // 4) * 128, 128)
    for t in range(3):
        loads.append(
            pltpu.make_async_copy(
                wqkv_hbm.at[:, pl.ds(t * 1024 + window, 128)], w3.at[t], local_sem.at[3 + t]
            )
        )
    for src, dst in (
        (inner_hbm.at[0], inner_ref), (outer_hbm.at[0], outer_ref), (adj_hbm.at[0], adj.at[0, pl.ds(0, 16)]),
        (adj_hbm.at[1], adj.at[1, pl.ds(0, 16)]), (nb_hbm, nb), (blocks_hbm, blocks), (counts_hbm, counts),
        (wo_hbm, wo), (wu_hbm, wu), (wd_hbm, wd),
    ):
        loads.append(pltpu.make_async_copy(src, dst, local_sem.at[len(loads)]))
    for i in (0, 1, 6):
        loads[i].start()
    loads[6].wait()
    idx[me, c, :, 0:64] = inner_ref[...]
    idx[me, c, :, 64:128] = jnp.zeros((32, 64), jnp.int32)
    loads[0].wait()
    loads[1].wait()
    pl.semaphore_wait(bar, 34)
    started = []

    class Route:
        def __init__(self, b):
            self.b = b
            self.p, self.s = (y, z) if b == 0 else (z, y)

        def chip(self, dp, ds):
            p, s = wrap(self.p + dp), wrap(self.s + ds)
            return p * 4 + s if self.b == 0 else s * 4 + p

        def target(self, dp, ds):
            p, s = wrap(self.p + dp), wrap(self.s + ds)
            return dev_of(p, s, c) if self.b == 0 else dev_of(s, p, c)

        def view(self, dp, ds, half):
            r = xall.at[self.chip(dp, ds), c, self.b]
            return r if half is None else r.at[pl.ds(half * 64, 64)]

        def copies(self, tag, dp, ds, half, to):
            v = self.view(dp, ds, half)
            k = self.b * 20 + tag
            out = [
                pltpu.make_async_remote_copy(
                    v, v, send_sem.at[k], recv_sem.at[k], device_id={"dev": to}, device_id_type=MESH
                )
            ]
            if self.b == 0 and half != 1:
                v = idx.at[self.chip(dp, ds), c]
                out.append(
                    pltpu.make_async_remote_copy(
                        v, v, isend.at[tag], irecv.at[tag], device_id={"dev": to}, device_id_type=MESH
                    )
                )
            return out

        def send(self, tag, dp, ds, half, to_p, to_s):
            for copy in self.copies(tag, dp, ds, half, self.target(to_p, to_s)):
                copy.start()
                started.append(copy)

        def wait(self, tag, dp, ds, half=None):
            for copy in self.copies(tag, dp, ds, half, sib):
                copy.wait_recv()

        def sib_copy(self, dp, ds):
            i = self.chip(dp, ds)
            v = self.view(dp, ds, None)
            copies = [
                pltpu.make_async_remote_copy(
                    v, v, sib_send.at[i * 2 + self.b], sib_recv.at[i * 2 + self.b],
                    device_id={"dev": sib}, device_id_type=MESH,
                )
            ]
            if self.b == 0:
                v = idx.at[i, c]
                copies.append(
                    pltpu.make_async_remote_copy(
                        v, v, sibi_send.at[i], sibi_recv.at[i],
                        device_id={"dev": sib}, device_id_type=MESH,
                    )
                )
            for copy in copies:
                copy.start()
                started.append(copy)

    def sib_wait(chip):
        for b in range(2):
            v = xall.at[chip, 1 - c, b]
            pltpu.make_async_remote_copy(
                v, v, sib_send.at[chip * 2 + b], sib_recv.at[chip * 2 + b],
                device_id={"dev": sib}, device_id_type=MESH,
            ).wait_recv()
        v = idx.at[chip, 1 - c]
        pltpu.make_async_remote_copy(
            v, v, sibi_send.at[chip], sibi_recv.at[chip],
            device_id={"dev": sib}, device_id_type=MESH,
        ).wait_recv()

    lane = lax.broadcasted_iota(jnp.int32, (256, 128), 1)
    row = lax.broadcasted_iota(jnp.int32, (256, 64), 0)

    def add_block(t, block):
        for b in range(2):
            at = 16
            for s in range(16):
                at = jnp.where(nb[b, s] == t, s, at)
            acc[b] += dot(adj[b, at], block)

    def process(chip):
        sib_wait(chip)
        for cc in range(2):
            rows = xall[chip, cc].reshape(256, 1024)
            both = dot(rows, wc[...])
            at = chip * 4 + cc * 2
            q[pl.ds(at, 2)] = both[:, :128].astype(BF).reshape(2, 128, 128)
            kv[pl.ds(at, 2)] = (
                jnp.where(lane == ONES_LANE, 1.0, both[:, 128:]).astype(BF).reshape(2, 128, 128)
            )
            picks = idx[chip, cc, pl.ds(d, 1), :][:, 0:64]
            hot = jnp.where(row == picks, 1.0, 0.0).astype(BF)
            xsel[pl.ds(cc * 64, 64), :] = dot_tn(hot, rows).astype(BF)
        add_block(2 + chip, dot(xsel[...], wg[...]).astype(BF))

    def process_many(count, where):
        def step(i, carry):
            dy, dz = where(i)
            process(wrap(y + dy) * 4 + wrap(z + dz))
            return carry

        lax.fori_loop(0, count, step, 0)

    routes = [Route(0), Route(1)]
    for t in routes:
        t.send(0, 0, 0, None, 1, 0)
        t.send(1, 0, 0, None, -1, 0)
    for t in routes:
        t.send(4, 0, 0, None, 0, 1)
        t.send(5, 0, 0, None, 0, -1)
    for t in routes:
        t.sib_copy(0, 0)

    for i in (2, 3, 4, 5, 7, 8, 9, 10, 11, 12, 13, 14, 15):
        loads[i].start()

    loads[2].wait()
    own = dot(xall[me, c].reshape(256, 1024), wg[...]).astype(BF)
    loads[7].wait()
    for r in range(1, 4):
        to = wrap(g + r)
        hot = jnp.where(
            lax.broadcasted_iota(jnp.int32, (256, 128), 0) == outer_ref[pl.ds(to, 1), :], 1.0, 0.0
        ).astype(BF)
        outsel[r - 1] = dot_tn(hot, own).astype(BF)
        copy = pltpu.make_async_remote_copy(
            outsel.at[r - 1], outin.at[r - 1], out_send.at[r - 1], out_recv.at[r - 1],
            device_id={"group": to}, device_id_type=MESH,
        )
        copy.start()
        started.append(copy)

    for t in range(3):
        loads[3 + t].wait()
    take = lax.broadcasted_iota(jnp.int32, (128, 256), 0) - (d % 4) * HEAD
    col = lax.broadcasted_iota(jnp.int32, (128, 256), 1)
    total = jnp.zeros((1024, 256), F32)
    for t in range(3):
        first = (0, 128, 128 + HEAD)[t]
        inside = (take >= 0) & (take < HEAD) & (col == take + first)
        total = total + dot(w3[t], jnp.where(inside, 1.0, 0.0).astype(BF))
    wc[...] = total.astype(BF)

    def e1():
        for t in routes:
            t.wait(0, -1, 0)
            t.send(2, -1, 0, 0, 1, 0)
            t.wait(1, 1, 0)
            t.send(3, 1, 0, 1, -1, 0)
        for t in routes:
            for k in (1, 2):
                t.send(4 + 4 * k, STEPS[k], 0, None, 0, 1)
                t.send(5 + 4 * k, STEPS[k], 0, None, 0, -1)
                t.sib_copy(STEPS[k], 0)

    def e2():
        for t in routes:
            t.wait(2, 2, 0, 0)
            t.wait(3, 2, 0, 1)
            t.send(16, 2, 0, None, 0, 1)
            t.send(17, 2, 0, None, 0, -1)
            t.sib_copy(2, 0)

    def e3(k):
        for t in routes:
            t.wait(4 + 4 * k, STEPS[k], -1)
            t.send(6 + 4 * k, STEPS[k], -1, 0, 0, 1)
            t.wait(5 + 4 * k, STEPS[k], 1)
            t.send(7 + 4 * k, STEPS[k], 1, 1, 0, -1)
            t.sib_copy(STEPS[k], -1)
            t.sib_copy(STEPS[k], 1)

    def e4(k):
        for t in routes:
            t.wait(6 + 4 * k, STEPS[k], 2, 0)
            t.wait(7 + 4 * k, STEPS[k], 2, 1)
            t.sib_copy(STEPS[k], 2)

    def sign(i):
        return 1 - 2 * (i % 2)

    def own_blocks():
        for i in (8, 9, 10):
            loads[i].wait()
        for b in range(2):
            adj[b, 16] = jnp.zeros((128, 128), BF)
            acc[b] = jnp.zeros((128, 1024), F32)
        add_block(0, own[0:128])
        add_block(1, own[128:256])
        hot = jnp.where(
            lax.broadcasted_iota(jnp.int32, (256, 128), 0) == outer_ref[pl.ds(g, 1), :], 1.0, 0.0
        ).astype(BF)
        add_block(18 + g, dot_tn(hot, own).astype(BF))

    def outer_blocks():
        for r in range(1, 4):
            pltpu.make_async_remote_copy(
                outsel.at[r - 1], outin.at[r - 1], out_send.at[r - 1], out_recv.at[r - 1],
                device_id={"group": wrap(g + r)}, device_id_type=MESH,
            ).wait_recv()
            add_block(18 + wrap(g - r), outin[r - 1])

    own_blocks()
    e1()
    process_many(1, lambda i: (0 * i, 0 * i))
    e2()
    e3(0)
    process_many(2, lambda i: (sign(i), 0 * i))
    e3(1)
    process_many(2, lambda i: (0 * i, sign(i)))
    e3(2)
    outer_blocks()
    e3(3)
    process_many(4, lambda i: (sign(i), 1 - 2 * (i // 2)))
    e4(0)
    process_many(2, lambda i: (2 * i, 2 * (1 - i)))
    e4(1)
    process_many(2, lambda i: (3 * i - 1, 2 - 3 * i))
    e4(2)
    process_many(2, lambda i: (1 + i, 2 - i))
    e4(3)
    process_many(1, lambda i: (2 + 0 * i, 2 + 0 * i))
    kv[64] = jnp.zeros((128, 128), BF)

    factor = 1.4426950408889634 / HEAD**0.5
    slots = 16
    loads[11].wait()
    loads[12].wait()

    def score(i, scores, tops):
        query = q[i]
        highest = None
        for s in range(0, slots, 2):
            keys = [
                kv[jnp.where(s + u < counts[i], blocks[i, s + u], blocks[i, 0])] for u in range(2)
            ]
            part = dot_nt(query, jnp.concatenate(keys, axis=0))
            scores[:, pl.ds(s * 128, 256)] = part
            part = jnp.maximum(part[:, :128], part[:, 128:])
            highest = part if highest is None else jnp.maximum(highest, part)
        tops[...] = jnp.broadcast_to(jnp.max(highest, axis=1, keepdims=True) * factor, (128, 128))

    def mix(i, to, lanes, scores, tops):
        top = jnp.concatenate([tops[...]] * 2, axis=1)
        mixed = None
        for s in range(0, slots, 2):
            probs = jnp.exp2(scores[:, pl.ds(s * 128, 256)] * factor - top).astype(BF)
            values = [kv[jnp.where(s + u < counts[i], blocks[i, s + u], 64)] for u in range(2)]
            part = dot(probs, jnp.concatenate(values, axis=0))
            mixed = part if mixed is None else mixed + part
        turned = mixed.T
        part = turned[HEAD : 2 * HEAD] / turned[ONES_LANE : ONES_LANE + 1]
        ob[to, :, lanes * 128 : lanes * 128 + 128] = part.astype(BF)

    def give(r):
        return pltpu.make_async_remote_copy(
            ob.at[other(r)], ret.at[d], ret_send.at[r], ret_recv.at[r],
            device_id={"dev": other(r)}, device_id_type=MESH,
        )

    def take_in(r):
        return pltpu.make_async_remote_copy(
            ob.at[other(r)], ret.at[source(r)], ret_send.at[r], ret_recv.at[r],
            device_id={"dev": other(r)}, device_id_type=MESH,
        )

    score(other(31) * 2, s_a, m_a)

    def attend(n, carry):
        r = 31 - n
        to = other(r)
        score(to * 2 + 1, s_b, m_b)
        mix(to * 2, to, 0, s_a, m_a)
        score(other((r + 31) % 32) * 2, s_a, m_a)
        mix(to * 2 + 1, to, 1, s_b, m_b)

        @pl.when(r > 0)
        def _():
            give(r).start()

        return carry

    lax.fori_loop(0, 32, attend, 0)
    ret[d] = ob[d]
    features = xall[me, c].reshape(256, 1024).astype(F32)
    local = layer_norm(features + acc[...].reshape(256, 1024))
    loads[13].wait()

    def land(r, carry):
        take_in(r).wait_recv()
        return carry

    lax.fori_loop(1, 32, land, 0)
    projected = dot_tn(ret[...].reshape(1024, 256), wo[...])
    summed = local + layer_norm(features + projected)
    acc[...] = summed.reshape(2, 128, 1024)
    loads[14].wait()
    hidden = jax.nn.gelu(dot(summed.astype(BF), wu[...])).astype(BF)
    loads[15].wait()
    o_ref[...] = layer_norm(acc[...].reshape(256, 1024) + dot(hidden, wd[...])).astype(BF)

    for copy in started:
        copy.wait_send()

    def leave(r, carry):
        give(r).wait_send()
        return carry

    lax.fori_loop(1, 32, leave, 0)


def per_device(
    node_feats, w_gcn, adj_tiles, neighbor_blocks, inner_rows, outer_rows,
    w_qkv, key_blocks, key_counts, w_out, w_up, w_down,
):
    hbm = pl.BlockSpec(memory_space=pl.ANY)
    dma = pltpu.SemaphoreType.DMA
    return pl.pallas_call(
        layer_kernel,
        out_shape=jax.ShapeDtypeStruct((256, 1024), BF),
        in_specs=[hbm] * 12,
        out_specs=pl.BlockSpec(memory_space=pltpu.VMEM),
        scratch_shapes=[
            pltpu.VMEM((16, 2, 2, 128, 1024), BF),
            pltpu.VMEM((16, 2, 32, 128), jnp.int32),
            pltpu.VMEM((1024, 1024), BF),
            pltpu.VMEM((3, 1024, 128), BF),
            pltpu.VMEM((1024, 256), BF),
            pltpu.VMEM((128, 1024), BF),
            pltpu.VMEM((64, 128, 128), BF),
            pltpu.VMEM((65, 128, 128), BF),
            pltpu.VMEM((3, 128, 1024), BF),
            pltpu.VMEM((3, 128, 1024), BF),
            pltpu.VMEM((32, 64), jnp.int32),
            pltpu.VMEM((4, 128), jnp.int32),
            pltpu.VMEM((2, 17, 128, 128), BF),
            pltpu.VMEM((2, 128, 1024), F32),
            pltpu.VMEM((1024, 1024), BF),
            pltpu.VMEM((1024, 2048), BF),
            pltpu.VMEM((2048, 1024), BF),
            pltpu.VMEM((32, 32, 256), BF),
            pltpu.VMEM((32, 32, 256), BF),
            pltpu.VMEM((128, 2048), F32),
            pltpu.VMEM((128, 2048), F32),
            pltpu.VMEM((128, 128), F32),
            pltpu.VMEM((128, 128), F32),
            pltpu.SMEM((2, 16), jnp.int32),
            pltpu.SMEM((64, 16), jnp.int32),
            pltpu.SMEM((64,), jnp.int32),
            dma((40,)), dma((40,)), dma((20,)), dma((20,)), dma((32,)), dma((32,)), dma((16,)), dma((16,)),
            dma((3,)), dma((3,)), dma((16,)), dma((32,)), dma((32,)),
        ],
        compiler_params=pltpu.CompilerParams(
            collective_id=0, has_side_effects=True, vmem_limit_bytes=56 << 20
        ),
        name="layer",
    )(
        node_feats, w_gcn, w_qkv, inner_rows, outer_rows, adj_tiles, neighbor_blocks,
        key_blocks, key_counts, w_out, w_up, w_down,
    )


def solution(mesh):
    placed = (
        P(("group", "dev"), None),
        P(),
        P(("group", "dev"), None, None, None),
        P(("group", "dev"), None),
        P(("group", "dev"), None, None),
        P(("group", "dev"), None, None),
        P(),
        P("group", None),
        P("group"),
        P(),
        P(),
        P(),
    )
    return jax.shard_map(
        per_device, mesh=mesh, in_specs=placed, out_specs=P(("group", "dev"), None), check_vma=False
    )
```

```python
import jax
import jax.numpy as jnp
from jax import lax
from jax.experimental import pallas as pl
from jax.experimental.pallas import tpu as pltpu
from jax.sharding import PartitionSpec as P

MESH = pl.DeviceIdType.MESH
BF = jnp.bfloat16
F32 = jnp.float32
HEADS = 32
HEAD = 32
RING = 4
HALF = 512


def wrap(v):
    return (v + RING) % RING


def place():
    d = lax.axis_index("dev")
    return d, d // 8, (d // 2) % 4, d % 2


def dev_of(y, z, c):
    return y * 8 + z * 2 + c


def dot(a, b):
    return jnp.dot(a, b, preferred_element_type=F32)


def dot_nt(a, b):
    return lax.dot_general(a, b, (((1,), (1,)), ((), ())), preferred_element_type=F32)


def dot_tn(a, b):
    return lax.dot_general(a, b, (((0,), (0,)), ((), ())), preferred_element_type=F32)


def layer_norm(values):
    average = jnp.mean(values, axis=-1, keepdims=True)
    centered = values - average
    variance = jnp.mean(centered * centered, axis=-1, keepdims=True)
    return centered / jnp.sqrt(variance + 1e-05)


def layer_kernel(
    x_hbm, wg_hbm, wqkv_hbm, inner_hbm, outer_hbm, adj_hbm, nb_hbm, blocks_hbm, counts_hbm,
    wo_hbm, wu_hbm, wd_hbm,
    o_ref,
    x, wg, w, heads, qkv, query, value, own, ring, idx, picked, inner, outsel, outin, inner_ref, outer_ref, adj, acc,
    wo, wu, wd, ob, ret, s_a, s_b, m_a, m_b, nb, blocks, counts,
    qkv_send, qkv_recv, ring_send, ring_recv, idx_send, idx_recv, pick_send, pick_recv,
    out_send, out_recv, local_sem, w_sem, ret_send, ret_recv,
):
    d, y, z, c = place()
    g = lax.axis_index("group")
    bar = pltpu.get_barrier_semaphore()

    def other(r):
        return dev_of(wrap(y + r // 8), wrap(z + (r // 2) % 4), (c + r % 2) % 2)

    def source(r):
        return dev_of(wrap(y - r // 8), wrap(z - (r // 2) % 4), (c + r % 2) % 2)

    def hail(r, carry):
        pl.semaphore_signal(bar, inc=1, device_id={"dev": other(r)}, device_id_type=MESH)
        return carry

    lax.fori_loop(1, 32, hail, 0)
    for r in range(1, 4):
        pl.semaphore_signal(bar, inc=1, device_id={"group": wrap(g + r)}, device_id_type=MESH)

    pairs = (
        (x_hbm, x), (wg_hbm, wg), (inner_hbm.at[0], inner_ref), (outer_hbm.at[0], outer_ref),
        (adj_hbm.at[0], adj.at[0, pl.ds(0, 16)]), (adj_hbm.at[1], adj.at[1, pl.ds(0, 16)]),
        (nb_hbm, nb), (blocks_hbm, blocks), (counts_hbm, counts),
        (wo_hbm, wo), (wu_hbm, wu), (wd_hbm, wd),
    )
    loads = [
        pltpu.make_async_copy(src, dst, local_sem.at[i]) for i, (src, dst) in enumerate(pairs)
    ]

    def window(n):
        return (d // 4 + 3 * n) % 8

    def w_load(n, t):
        at = pl.multiple_of(t * 1024 + window(n) * 128, 128)
        return pltpu.make_async_copy(
            wqkv_hbm.at[:, pl.ds(at, 128)], w.at[n, :, pl.ds(t * 128, 128)], w_sem.at[n * 3 + t]
        )

    for load in loads[:4]:
        load.start()
    for n in range(8):
        for t in range(3):
            w_load(n, t).start()
    for load in loads[4:9]:
        load.start()
    tail = jnp.where(lax.broadcasted_iota(jnp.int32, (16, 128), 0) == 0, 1.0, 0.0).astype(BF)
    for i in range(64):
        qkv[i, 96:112, :] = tail
    loads[0].wait()
    pl.semaphore_wait(bar, 34)

    def qkv_copy(to):
        return pltpu.make_async_remote_copy(
            heads.at[to], qkv.at[pl.ds(2 * d, 2), pl.ds(0, 96)], qkv_send.at[to], qkv_recv.at[d],
            device_id={"dev": to}, device_id_type=MESH,
        )

    def qkv_land(src):
        return pltpu.make_async_remote_copy(
            heads.at[src], qkv.at[pl.ds(2 * src, 2), pl.ds(0, 96)], qkv_send.at[src], qkv_recv.at[src],
            device_id={"dev": src}, device_id_type=MESH,
        )

    def project(n, carry):
        for t in range(3):
            w_load(n, t).wait()
        turned = dot(x[...], w[n]).T.astype(BF)
        for k in range(4):
            to = window(n) * 4 + k
            for t in range(3):
                rows = turned[t * 128 + k * 32 : t * 128 + k * 32 + 32]
                for b in range(2):
                    heads[to, b, t * 32 : t * 32 + 32, :] = rows[:, b * 128 : b * 128 + 128]

            @pl.when(to != d)
            def _():
                qkv_copy(to).start()

        return carry

    loads[1].wait()
    own[...] = dot(x[...], wg[...]).astype(BF)
    loads[2].wait()
    lists = [inner_ref[pl.ds(k, 16, 2), :] for k in range(2)]

    class Route:
        def __init__(self, h):
            self.h = h
            self.p, self.s = (z, y) if h == 0 else (y, z)

        def chip(self, p, s):
            return s * 4 + p if self.h == 0 else p * 4 + s

        def target(self, dp, ds, cc):
            return self.chip(wrap(self.p + dp), wrap(self.s + ds)) * 2 + cc

        def copies(self, tag, dp, half, to):
            v = ring.at[self.h, wrap(self.p + dp)]
            if half is not None:
                v = v.at[pl.ds(half * 128, 128)]
            k = self.h * 4 + tag
            out = [
                pltpu.make_async_remote_copy(
                    v, v, ring_send.at[k], ring_recv.at[k], device_id={"dev": to}, device_id_type=MESH
                )
            ]
            if tag < 3:
                v = idx.at[self.h, wrap(self.p + dp)]
                out.append(
                    pltpu.make_async_remote_copy(
                        v, v, idx_send.at[k], idx_recv.at[k], device_id={"dev": to}, device_id_type=MESH
                    )
                )
            return out

        def send(self, tag, dp, half, to_p):
            for copy in self.copies(tag, dp, half, self.target(to_p, 0, c)):
                copy.start()
                started.append(copy)

        def wait(self, tag, dp, half=None):
            for copy in self.copies(tag, dp, half, self.target(1, 0, c)):
                copy.wait_recv()

        def pick(self, dp, ds):
            p = wrap(self.p + dp)
            row = self.chip(self.p, wrap(self.s + ds))
            hot = jnp.where(
                lax.broadcasted_iota(jnp.int32, (256, 128), 0) == idx[self.h, p, pl.ds(row, 1), :],
                1.0, 0.0,
            ).astype(BF)
            rows = dot_tn(hot, ring[self.h, p]).astype(BF)
            for cc in range(2):
                picked[self.h, ds, cc, p] = rows[cc * 64 : cc * 64 + 64]

        def pick_copy(self, ds, dc):
            cc = (c + dc) % 2
            k = self.h * 8 + ds * 2 + dc
            return pltpu.make_async_remote_copy(
                picked.at[self.h, ds, cc], inner.at[self.h, self.s, c], pick_send.at[k], pick_recv.at[k],
                device_id={"dev": self.target(0, ds, cc)}, device_id_type=MESH,
            )

        def pick_land(self, ds, dc):
            cc = (c + dc) % 2
            k = self.h * 8 + ds * 2 + dc
            return pltpu.make_async_remote_copy(
                picked.at[self.h, ds, cc], inner.at[self.h, wrap(self.s - ds), cc],
                pick_send.at[k], pick_recv.at[k],
                device_id={"dev": self.target(0, ds, cc)}, device_id_type=MESH,
            )

    started = []
    routes = [Route(0), Route(1)]
    for t in routes:
        ring[t.h, t.p] = own[:, t.h * HALF : t.h * HALF + HALF]
        idx[t.h, t.p, :, 0:64] = lists[0]
        idx[t.h, t.p, :, 64:128] = lists[1]
    for t in routes:
        t.send(0, 0, None, 1)
        t.send(1, 0, None, -1)

    lax.fori_loop(0, 8, project, 0)
    for load in loads[9:]:
        load.start()

    def outer_rows(to):
        hot = jnp.where(
            lax.broadcasted_iota(jnp.int32, (256, 128), 0) == outer_ref[pl.ds(to, 1), :], 1.0, 0.0
        ).astype(BF)
        return dot_tn(hot, own[...]).astype(BF)

    def outer_copy(r):
        return pltpu.make_async_remote_copy(
            outsel.at[r - 1], outin.at[r - 1], out_send.at[r - 1], out_recv.at[r - 1],
            device_id={"group": wrap(g + r)}, device_id_type=MESH,
        )

    loads[3].wait()
    for r in range(1, 4):
        outsel[r - 1] = outer_rows(wrap(g + r))
        outer_copy(r).start()
        started.append(outer_copy(r))

    def picks(t, count, where):
        def step(i, carry):
            t.pick(*where(i))
            return carry

        lax.fori_loop(0, count, step, 0)

    for t in routes:
        picks(t, 4, lambda i: (0 * i, i))

    def add_block(t, block):
        for b in range(2):
            at = 16
            for s in range(16):
                at = jnp.where(nb[b, s] == t, s, at)
            acc[b] += dot(adj[b, at], block)

    for i in (4, 5, 6):
        loads[i].wait()
    for b in range(2):
        adj[b, 16] = jnp.zeros((128, 128), BF)
        acc[b] = jnp.zeros((128, 1024), F32)
    add_block(0, own[0:128, :])
    add_block(1, own[128:256, :])
    add_block(18 + g, outer_rows(g))

    for t in routes:
        t.wait(0, -1)
        t.send(2, -1, 0, 1)
        t.wait(1, 1)
        t.send(3, 1, 1, -1)
    for t in routes:
        picks(t, 8, lambda i: (1 - 2 * (i // 4), i % 4))
    for t in routes:
        t.wait(2, 2, 0)
        t.wait(3, 2, 1)
        picks(t, 4, lambda i: (2 + 0 * i, i))
    for t in routes:
        inner[t.h, t.s, c] = picked[t.h, 0, c]
    for r in range(1, 4):
        outer_copy(r).wait_recv()
        add_block(18 + wrap(g - r), outin[r - 1])

    qkv[pl.ds(2 * d, 2), pl.ds(0, 96)] = heads[d]

    def turn(src):
        for b in range(2):
            i = 2 * src + b
            query[i] = qkv[i, 0:32, :].astype(F32).T.astype(BF)
            value[i] = qkv[i, 64:112, :].astype(F32).T.astype(BF)

    turn(d)
    value[64] = jnp.zeros((128, 48), BF)

    def arrive(n, carry):
        src = source((5 * n) % 32)
        qkv_land(src).wait_recv()
        turn(src)
        return carry

    lax.fori_loop(1, 32, arrive, 0)
    hops = [(2, 0), (2, 1), (1, 0), (1, 1), (3, 0), (3, 1), (0, 1)]
    for ds, dc in hops:
        for t in routes:
            t.pick_copy(ds, dc).start()

    factor = 1.4426950408889634 / HEAD**0.5
    slots = 16
    loads[7].wait()
    loads[8].wait()

    def score(i, scores, tops):
        highest = None
        for s in range(0, slots, 2):
            keys = [
                qkv[jnp.where(s + u < counts[i], blocks[s + u, i], blocks[0, i]), 32:64, :]
                for u in range(2)
            ]
            part = dot(query[i], jnp.concatenate(keys, axis=1))
            scores[:, pl.ds(s * 128, 256)] = part
            part = jnp.maximum(part[:, :128], part[:, 128:])
            highest = part if highest is None else jnp.maximum(highest, part)
        tops[...] = jnp.broadcast_to(jnp.max(highest, axis=1, keepdims=True) * factor, (128, 128))

    def mix(i, to, lanes, scores, tops):
        top = jnp.concatenate([tops[...]] * 2, axis=1)
        mixed = None
        for s in range(0, slots, 2):
            probs = jnp.exp2(scores[:, pl.ds(s * 128, 256)] * factor - top).astype(BF)
            values = [
                value[jnp.where(s + u < counts[i], blocks[s + u, i], 64)] for u in range(2)
            ]
            part = dot(probs, jnp.concatenate(values, axis=0))
            mixed = part if mixed is None else mixed + part
        mixed = mixed.T
        part = mixed[0:32] / mixed[32:33]
        ob[to, :, lanes * 128 : lanes * 128 + 128] = part.astype(BF)

    def give(r):
        return pltpu.make_async_remote_copy(
            ob.at[other(r)], ret.at[d], ret_send.at[r], ret_recv.at[r],
            device_id={"dev": other(r)}, device_id_type=MESH,
        )

    def take_in(r):
        return pltpu.make_async_remote_copy(
            ob.at[other(r)], ret.at[source(r)], ret_send.at[r], ret_recv.at[r],
            device_id={"dev": other(r)}, device_id_type=MESH,
        )

    score(other(31) * 2, s_a, m_a)

    def attend(n, carry):
        r = 31 - n
        to = other(r)
        score(to * 2 + 1, s_b, m_b)
        mix(to * 2, to, 0, s_a, m_a)
        score(other((r + 31) % 32) * 2, s_a, m_a)
        mix(to * 2 + 1, to, 1, s_b, m_b)

        @pl.when(r > 0)
        def _():
            give(r).start()

        return carry

    lax.fori_loop(0, 32, attend, 0)
    ret[d] = ob[d]

    for ds, dc in reversed(hops):
        for t in routes:
            t.pick_land(ds, dc).wait_recv()

    def gathered(row, carry):
        parts = []
        for col in range(4):
            left = inner[0, row, :, col].reshape(128, HALF)
            right = inner[1, col, :, row].reshape(128, HALF)
            parts.append(jnp.concatenate([left, right], axis=1))
        table = jnp.concatenate(parts, axis=0)
        for b in range(2):
            tiles = []
            for col in range(4):
                at = 16
                for s in range(16):
                    at = jnp.where(nb[b, s] == 2 + row * 4 + col, s, at)
                tiles.append(adj[b, at])
            acc[b] += dot(jnp.concatenate(tiles, axis=1), table)
        return carry

    lax.fori_loop(0, 4, gathered, 0)
    features = x[...].astype(F32)
    local = layer_norm(features + acc[...].reshape(256, 1024))
    loads[9].wait()

    def land(r, carry):
        take_in(r).wait_recv()
        return carry

    lax.fori_loop(1, 32, land, 0)
    projected = dot_tn(ret[...].reshape(1024, 256), wo[...])
    summed = local + layer_norm(features + projected)
    acc[...] = summed.reshape(2, 128, 1024)
    loads[10].wait()
    hidden = jax.nn.gelu(dot(summed.astype(BF), wu[...])).astype(BF)
    loads[11].wait()
    o_ref[...] = layer_norm(acc[...].reshape(256, 1024) + dot(hidden, wd[...])).astype(BF)

    for copy in started:
        copy.wait_send()
    for ds, dc in hops:
        for t in routes:
            t.pick_copy(ds, dc).wait_send()

    def leave(r, carry):
        give(r).wait_send()
        qkv_copy((d + r) % 32).wait_send()
        return carry

    lax.fori_loop(1, 32, leave, 0)


def per_device(
    node_feats, w_gcn, adj_tiles, neighbor_blocks, inner_rows, outer_rows,
    w_qkv, key_blocks, key_counts, w_out, w_up, w_down,
):
    hbm = pl.BlockSpec(memory_space=pl.ANY)
    dma = pltpu.SemaphoreType.DMA
    return pl.pallas_call(
        layer_kernel,
        out_shape=jax.ShapeDtypeStruct((256, 1024), BF),
        in_specs=[hbm] * 12,
        out_specs=pl.BlockSpec(memory_space=pltpu.VMEM),
        scratch_shapes=[
            pltpu.VMEM((256, 1024), BF),
            pltpu.VMEM((1024, 1024), BF),
            pltpu.VMEM((8, 1024, 384), BF),
            pltpu.VMEM((32, 2, 96, 128), BF),
            pltpu.VMEM((64, 112, 128), BF),
            pltpu.VMEM((64, 128, 32), BF),
            pltpu.VMEM((65, 128, 48), BF),
            pltpu.VMEM((256, 1024), BF),
            pltpu.VMEM((2, 4, 256, HALF), BF),
            pltpu.VMEM((2, 4, 16, 128), jnp.int32),
            pltpu.VMEM((2, 4, 2, 4, 64, HALF), BF),
            pltpu.VMEM((2, 4, 2, 4, 64, HALF), BF),
            pltpu.VMEM((3, 128, 1024), BF),
            pltpu.VMEM((3, 128, 1024), BF),
            pltpu.VMEM((32, 64), jnp.int32),
            pltpu.VMEM((4, 128), jnp.int32),
            pltpu.VMEM((2, 17, 128, 128), BF),
            pltpu.VMEM((2, 128, 1024), F32),
            pltpu.VMEM((1024, 1024), BF),
            pltpu.VMEM((1024, 2048), BF),
            pltpu.VMEM((2048, 1024), BF),
            pltpu.VMEM((32, 32, 256), BF),
            pltpu.VMEM((32, 32, 256), BF),
            pltpu.VMEM((128, 2048), F32),
            pltpu.VMEM((128, 2048), F32),
            pltpu.VMEM((128, 128), F32),
            pltpu.VMEM((128, 128), F32),
            pltpu.SMEM((2, 16), jnp.int32),
            pltpu.SMEM((16, 64), jnp.int32),
            pltpu.SMEM((64,), jnp.int32),
            dma((32,)), dma((32,)), dma((8,)), dma((8,)), dma((8,)), dma((8,)), dma((16,)), dma((16,)),
            dma((3,)), dma((3,)), dma((12,)), dma((24,)), dma((32,)), dma((32,)),
        ],
        compiler_params=pltpu.CompilerParams(
            collective_id=0, has_side_effects=True, vmem_limit_bytes=58 << 20
        ),
        name="layer",
    )(
        node_feats, w_gcn, w_qkv, inner_rows, outer_rows, adj_tiles, neighbor_blocks,
        key_blocks.T, key_counts, w_out, w_up, w_down,
    )


def solution(mesh):
    placed = (
        P(("group", "dev"), None),
        P(),
        P(("group", "dev"), None, None, None),
        P(("group", "dev"), None),
        P(("group", "dev"), None, None),
        P(("group", "dev"), None, None),
        P(),
        P("group", None),
        P("group"),
        P(),
        P(),
        P(),
    )
    return jax.shard_map(
        per_device, mesh=mesh, in_specs=placed, out_specs=P(("group", "dev"), None), check_vma=False
    )
```

```python
import jax
import jax.numpy as jnp
from jax import lax
from jax.experimental import pallas as pl
from jax.experimental.pallas import tpu as pltpu
from jax.sharding import PartitionSpec as P

MESH = pl.DeviceIdType.MESH
BF = jnp.bfloat16
F32 = jnp.float32
HEADS = 32
HEAD = 32
RING = 4
HALF = 512


def wrap(v):
    return (v + RING) % RING


def place():
    d = lax.axis_index("dev")
    return d, d // 8, (d // 2) % 4, d % 2


def dev_of(y, z, c):
    return y * 8 + z * 2 + c


def dot(a, b):
    return jnp.dot(a, b, preferred_element_type=F32)


def dot_nt(a, b):
    return lax.dot_general(a, b, (((1,), (1,)), ((), ())), preferred_element_type=F32)


def dot_tn(a, b):
    return lax.dot_general(a, b, (((0,), (0,)), ((), ())), preferred_element_type=F32)


def layer_norm(values):
    average = jnp.mean(values, axis=-1, keepdims=True)
    centered = values - average
    variance = jnp.mean(centered * centered, axis=-1, keepdims=True)
    return centered / jnp.sqrt(variance + 1e-05)


def layer_kernel(
    x_hbm, wg_hbm, wqkv_hbm, inner_hbm, outer_hbm, adj_hbm, nb_hbm, blocks_hbm, counts_hbm,
    wo_hbm, wu_hbm, wd_hbm,
    o_ref,
    x, wg, w, heads, qkv, query, value, own, ring, idx, picked, inner, outsel, outin, inner_ref, outer_ref, adj, acc,
    wo, wu, wd, ob, ret, s_a, s_b, m_a, m_b, nb, blocks, counts,
    qkv_send, qkv_recv, ring_send, ring_recv, idx_send, idx_recv, pick_send, pick_recv,
    out_send, out_recv, local_sem, w_sem, ret_send, ret_recv,
):
    d, y, z, c = place()
    g = lax.axis_index("group")
    bar = pltpu.get_barrier_semaphore()

    def other(r):
        return dev_of(wrap(y + r // 8), wrap(z + (r // 2) % 4), (c + r % 2) % 2)

    def source(r):
        return dev_of(wrap(y - r // 8), wrap(z - (r // 2) % 4), (c + r % 2) % 2)

    def hail(r, carry):
        pl.semaphore_signal(bar, inc=1, device_id={"dev": other(r)}, device_id_type=MESH)
        return carry

    lax.fori_loop(1, 32, hail, 0)
    for r in range(1, 4):
        pl.semaphore_signal(bar, inc=1, device_id={"group": wrap(g + r)}, device_id_type=MESH)

    pairs = (
        (x_hbm, x), (wg_hbm, wg), (inner_hbm.at[0], inner_ref), (outer_hbm.at[0], outer_ref),
        (adj_hbm.at[0], adj.at[0, pl.ds(0, 16)]), (adj_hbm.at[1], adj.at[1, pl.ds(0, 16)]),
        (nb_hbm, nb), (blocks_hbm, blocks), (counts_hbm, counts),
        (wo_hbm, wo), (wu_hbm, wu), (wd_hbm, wd),
    )
    loads = [
        pltpu.make_async_copy(src, dst, local_sem.at[i]) for i, (src, dst) in enumerate(pairs)
    ]

    def window(n):
        return (d // 4 + 5 * n) % 8

    def w_load(n, t):
        at = pl.multiple_of(t * 1024 + window(n) * 128, 128)
        return pltpu.make_async_copy(
            wqkv_hbm.at[:, pl.ds(at, 128)], w.at[n, :, pl.ds(t * 128, 128)], w_sem.at[n * 3 + t]
        )

    for load in loads[:4]:
        load.start()
    for n in range(8):
        for t in range(3):
            w_load(n, t).start()
    for load in loads[4:9]:
        load.start()
    tail = jnp.where(lax.broadcasted_iota(jnp.int32, (16, 128), 0) == 0, 1.0, 0.0).astype(BF)
    for i in range(64):
        qkv[i, 96:112, :] = tail
    loads[0].wait()

    def qkv_copy(to):
        return pltpu.make_async_remote_copy(
            heads.at[to], qkv.at[pl.ds(2 * d, 2), pl.ds(0, 96)], qkv_send.at[to], qkv_recv.at[d],
            device_id={"dev": to}, device_id_type=MESH,
        )

    def qkv_land(src):
        return pltpu.make_async_remote_copy(
            heads.at[src], qkv.at[pl.ds(2 * src, 2), pl.ds(0, 96)], qkv_send.at[src], qkv_recv.at[src],
            device_id={"dev": src}, device_id_type=MESH,
        )

    def project(n, carry):
        for t in range(3):
            w_load(n, t).wait()
        turned = dot(x[...], w[n]).T.astype(BF)
        for k in range(4):
            to = window(n) * 4 + k
            for t in range(3):
                rows = turned[t * 128 + k * 32 : t * 128 + k * 32 + 32]
                for b in range(2):
                    heads[to, b, t * 32 : t * 32 + 32, :] = rows[:, b * 128 : b * 128 + 128]

            @pl.when(to != d)
            def _():
                qkv_copy(to).start()

        return carry

    loads[1].wait()
    own[...] = dot(x[...], wg[...]).astype(BF)
    loads[2].wait()
    lists = [inner_ref[pl.ds(k, 16, 2), :] for k in range(2)]

    class Route:
        def __init__(self, h):
            self.h = h
            self.p, self.s = (z, y) if h == 0 else (y, z)

        def chip(self, p, s):
            return s * 4 + p if self.h == 0 else p * 4 + s

        def target(self, dp, ds, cc):
            return self.chip(wrap(self.p + dp), wrap(self.s + ds)) * 2 + cc

        def copies(self, tag, dp, half, to):
            v = ring.at[self.h, wrap(self.p + dp)]
            if half is not None:
                v = v.at[pl.ds(half * 128, 128)]
            k = self.h * 4 + tag
            out = [
                pltpu.make_async_remote_copy(
                    v, v, ring_send.at[k], ring_recv.at[k], device_id={"dev": to}, device_id_type=MESH
                )
            ]
            if tag < 3:
                v = idx.at[self.h, wrap(self.p + dp)]
                out.append(
                    pltpu.make_async_remote_copy(
                        v, v, idx_send.at[k], idx_recv.at[k], device_id={"dev": to}, device_id_type=MESH
                    )
                )
            return out

        def send(self, tag, dp, half, to_p):
            for copy in self.copies(tag, dp, half, self.target(to_p, 0, c)):
                copy.start()
                started.append(copy)

        def wait(self, tag, dp, half=None):
            for copy in self.copies(tag, dp, half, self.target(1, 0, c)):
                copy.wait_recv()

        def pick(self, dp, ds):
            p = wrap(self.p + dp)
            row = self.chip(self.p, wrap(self.s + ds))
            hot = jnp.where(
                lax.broadcasted_iota(jnp.int32, (256, 128), 0) == idx[self.h, p, pl.ds(row, 1), :],
                1.0, 0.0,
            ).astype(BF)
            rows = dot_tn(hot, ring[self.h, p]).astype(BF)
            for cc in range(2):
                picked[self.h, ds, cc, p] = rows[cc * 64 : cc * 64 + 64]

        def pick_copy(self, ds, dc):
            cc = (c + dc) % 2
            k = self.h * 8 + ds * 2 + dc
            return pltpu.make_async_remote_copy(
                picked.at[self.h, ds, cc], inner.at[self.h, self.s, c], pick_send.at[k], pick_recv.at[k],
                device_id={"dev": self.target(0, ds, cc)}, device_id_type=MESH,
            )

        def pick_land(self, ds, dc):
            cc = (c + dc) % 2
            k = self.h * 8 + ds * 2 + dc
            return pltpu.make_async_remote_copy(
                picked.at[self.h, ds, cc], inner.at[self.h, wrap(self.s - ds), cc],
                pick_send.at[k], pick_recv.at[k],
                device_id={"dev": self.target(0, ds, cc)}, device_id_type=MESH,
            )

    started = []
    routes = [Route(0), Route(1)]
    for t in routes:
        ring[t.h, t.p] = own[:, t.h * HALF : t.h * HALF + HALF]
        idx[t.h, t.p, :, 0:64] = lists[0]
        idx[t.h, t.p, :, 64:128] = lists[1]
    pl.semaphore_wait(bar, 34)
    for t in routes:
        t.send(0, 0, None, 1)
        t.send(1, 0, None, -1)

    lax.fori_loop(0, 8, project, 0)
    for load in loads[9:]:
        load.start()

    def outer_rows(to):
        hot = jnp.where(
            lax.broadcasted_iota(jnp.int32, (256, 128), 0) == outer_ref[pl.ds(to, 1), :], 1.0, 0.0
        ).astype(BF)
        return dot_tn(hot, own[...]).astype(BF)

    def outer_copy(r):
        return pltpu.make_async_remote_copy(
            outsel.at[r - 1], outin.at[r - 1], out_send.at[r - 1], out_recv.at[r - 1],
            device_id={"group": wrap(g + r)}, device_id_type=MESH,
        )

    loads[3].wait()
    for r in range(1, 4):
        outsel[r - 1] = outer_rows(wrap(g + r))
        outer_copy(r).start()
        started.append(outer_copy(r))

    def picks(t, count, where):
        def step(i, carry):
            t.pick(*where(i))
            return carry

        lax.fori_loop(0, count, step, 0)

    for t in routes:
        picks(t, 4, lambda i: (0 * i, i))

    def add_block(t, block):
        for b in range(2):
            at = 16
            for s in range(16):
                at = jnp.where(nb[b, s] == t, s, at)
            acc[b] += dot(adj[b, at], block)

    for i in (4, 5, 6):
        loads[i].wait()
    for b in range(2):
        adj[b, 16] = jnp.zeros((128, 128), BF)
        acc[b] = jnp.zeros((128, 1024), F32)
    add_block(0, own[0:128, :])
    add_block(1, own[128:256, :])
    add_block(18 + g, outer_rows(g))

    for t in routes:
        t.wait(0, -1)
        t.send(2, -1, 0, 1)
        t.wait(1, 1)
        t.send(3, 1, 1, -1)
    for t in routes:
        picks(t, 8, lambda i: (1 - 2 * (i // 4), i % 4))
    for t in routes:
        t.wait(2, 2, 0)
        t.wait(3, 2, 1)
        picks(t, 4, lambda i: (2 + 0 * i, i))
    for t in routes:
        inner[t.h, t.s, c] = picked[t.h, 0, c]
    for r in range(1, 4):
        outer_copy(r).wait_recv()
        add_block(18 + wrap(g - r), outin[r - 1])

    hops = [(2, 0), (2, 1), (1, 0), (1, 1), (3, 0), (3, 1), (0, 1)]
    for ds, dc in hops:
        for t in routes:
            t.pick_copy(ds, dc).start()

    qkv[pl.ds(2 * d, 2), pl.ds(0, 96)] = heads[d]

    def turn(src):
        for b in range(2):
            i = 2 * src + b
            query[i] = qkv[i, 0:32, :].astype(F32).T.astype(BF)
            value[i] = qkv[i, 64:112, :].astype(F32).T.astype(BF)

    turn(d)
    value[64] = jnp.zeros((128, 48), BF)

    def arrive(n, carry):
        src = source((5 * n) % 32)
        qkv_land(src).wait_recv()
        turn(src)
        return carry

    lax.fori_loop(1, 32, arrive, 0)
    factor = 1.4426950408889634 / HEAD**0.5
    slots = 16
    loads[7].wait()
    loads[8].wait()

    def score(i, scores, tops):
        highest = None
        for s in range(0, slots, 2):
            keys = [
                qkv[jnp.where(s + u < counts[i], blocks[s + u, i], blocks[0, i]), 32:64, :]
                for u in range(2)
            ]
            part = dot(query[i], jnp.concatenate(keys, axis=1))
            scores[:, pl.ds(s * 128, 256)] = part
            part = jnp.maximum(part[:, :128], part[:, 128:])
            highest = part if highest is None else jnp.maximum(highest, part)
        tops[...] = jnp.broadcast_to(jnp.max(highest, axis=1, keepdims=True) * factor, (128, 128))

    def mix(i, to, lanes, scores, tops):
        top = jnp.concatenate([tops[...]] * 2, axis=1)
        mixed = None
        for s in range(0, slots, 2):
            probs = jnp.exp2(scores[:, pl.ds(s * 128, 256)] * factor - top).astype(BF)
            values = [
                value[jnp.where(s + u < counts[i], blocks[s + u, i], 64)] for u in range(2)
            ]
            part = dot(probs, jnp.concatenate(values, axis=0))
            mixed = part if mixed is None else mixed + part
        mixed = mixed.T
        part = mixed[0:32] / mixed[32:33]
        ob[to, :, lanes * 128 : lanes * 128 + 128] = part.astype(BF)

    def give(r):
        return pltpu.make_async_remote_copy(
            ob.at[other(r)], ret.at[d], ret_send.at[r], ret_recv.at[r],
            device_id={"dev": other(r)}, device_id_type=MESH,
        )

    def take_in(r):
        return pltpu.make_async_remote_copy(
            ob.at[other(r)], ret.at[source(r)], ret_send.at[r], ret_recv.at[r],
            device_id={"dev": other(r)}, device_id_type=MESH,
        )

    score(other(31) * 2, s_a, m_a)

    def attend(n, carry):
        r = 31 - n
        to = other(r)
        score(to * 2 + 1, s_b, m_b)
        mix(to * 2, to, 0, s_a, m_a)
        score(other((r + 31) % 32) * 2, s_a, m_a)
        mix(to * 2 + 1, to, 1, s_b, m_b)

        @pl.when(r > 0)
        def _():
            give(r).start()

        return carry

    lax.fori_loop(0, 32, attend, 0)
    ret[d] = ob[d]

    for ds, dc in reversed(hops):
        for t in routes:
            t.pick_land(ds, dc).wait_recv()

    def gathered(row, carry):
        parts = []
        for col in range(4):
            left = inner[0, row, :, col].reshape(128, HALF)
            right = inner[1, col, :, row].reshape(128, HALF)
            parts.append(jnp.concatenate([left, right], axis=1))
        table = jnp.concatenate(parts, axis=0)
        for b in range(2):
            tiles = []
            for col in range(4):
                at = 16
                for s in range(16):
                    at = jnp.where(nb[b, s] == 2 + row * 4 + col, s, at)
                tiles.append(adj[b, at])
            acc[b] += dot(jnp.concatenate(tiles, axis=1), table)
        return carry

    lax.fori_loop(0, 4, gathered, 0)
    features = x[...].astype(F32)
    local = layer_norm(features + acc[...].reshape(256, 1024))
    loads[9].wait()

    def land(r, carry):
        take_in(r).wait_recv()
        return carry

    lax.fori_loop(1, 32, land, 0)
    projected = dot_tn(ret[...].reshape(1024, 256), wo[...])
    summed = local + layer_norm(features + projected)
    acc[...] = summed.reshape(2, 128, 1024)
    loads[10].wait()
    hidden = jax.nn.gelu(dot(summed.astype(BF), wu[...])).astype(BF)
    loads[11].wait()
    o_ref[...] = layer_norm(acc[...].reshape(256, 1024) + dot(hidden, wd[...])).astype(BF)

    for copy in started:
        copy.wait_send()
    for ds, dc in hops:
        for t in routes:
            t.pick_copy(ds, dc).wait_send()

    def leave(r, carry):
        give(r).wait_send()
        qkv_copy((d + r) % 32).wait_send()
        return carry

    lax.fori_loop(1, 32, leave, 0)


def per_device(
    node_feats, w_gcn, adj_tiles, neighbor_blocks, inner_rows, outer_rows,
    w_qkv, key_blocks, key_counts, w_out, w_up, w_down,
):
    hbm = pl.BlockSpec(memory_space=pl.ANY)
    dma = pltpu.SemaphoreType.DMA
    return pl.pallas_call(
        layer_kernel,
        out_shape=jax.ShapeDtypeStruct((256, 1024), BF),
        in_specs=[hbm] * 12,
        out_specs=pl.BlockSpec(memory_space=pltpu.VMEM),
        scratch_shapes=[
            pltpu.VMEM((256, 1024), BF),
            pltpu.VMEM((1024, 1024), BF),
            pltpu.VMEM((8, 1024, 384), BF),
            pltpu.VMEM((32, 2, 96, 128), BF),
            pltpu.VMEM((64, 112, 128), BF),
            pltpu.VMEM((64, 128, 32), BF),
            pltpu.VMEM((65, 128, 48), BF),
            pltpu.VMEM((256, 1024), BF),
            pltpu.VMEM((2, 4, 256, HALF), BF),
            pltpu.VMEM((2, 4, 16, 128), jnp.int32),
            pltpu.VMEM((2, 4, 2, 4, 64, HALF), BF),
            pltpu.VMEM((2, 4, 2, 4, 64, HALF), BF),
            pltpu.VMEM((3, 128, 1024), BF),
            pltpu.VMEM((3, 128, 1024), BF),
            pltpu.VMEM((32, 64), jnp.int32),
            pltpu.VMEM((4, 128), jnp.int32),
            pltpu.VMEM((2, 17, 128, 128), BF),
            pltpu.VMEM((2, 128, 1024), F32),
            pltpu.VMEM((1024, 1024), BF),
            pltpu.VMEM((1024, 2048), BF),
            pltpu.VMEM((2048, 1024), BF),
            pltpu.VMEM((32, 32, 256), BF),
            pltpu.VMEM((32, 32, 256), BF),
            pltpu.VMEM((128, 2048), F32),
            pltpu.VMEM((128, 2048), F32),
            pltpu.VMEM((128, 128), F32),
            pltpu.VMEM((128, 128), F32),
            pltpu.SMEM((2, 16), jnp.int32),
            pltpu.SMEM((16, 64), jnp.int32),
            pltpu.SMEM((64,), jnp.int32),
            dma((32,)), dma((32,)), dma((8,)), dma((8,)), dma((8,)), dma((8,)), dma((16,)), dma((16,)),
            dma((3,)), dma((3,)), dma((12,)), dma((24,)), dma((32,)), dma((32,)),
        ],
        compiler_params=pltpu.CompilerParams(
            collective_id=0, has_side_effects=True, vmem_limit_bytes=58 << 20
        ),
        name="layer",
    )(
        node_feats, w_gcn, w_qkv, inner_rows, outer_rows, adj_tiles, neighbor_blocks,
        key_blocks.T, key_counts, w_out, w_up, w_down,
    )


def solution(mesh):
    placed = (
        P(("group", "dev"), None),
        P(),
        P(("group", "dev"), None, None, None),
        P(("group", "dev"), None),
        P(("group", "dev"), None, None),
        P(("group", "dev"), None, None),
        P(),
        P("group", None),
        P("group"),
        P(),
        P(),
        P(),
    )
    return jax.shard_map(
        per_device, mesh=mesh, in_specs=placed, out_specs=P(("group", "dev"), None), check_vma=False
    )
```

```python
import jax
import jax.numpy as jnp
from jax import lax
from jax.experimental import pallas as pl
from jax.experimental.pallas import tpu as pltpu
from jax.sharding import PartitionSpec as P

MESH = pl.DeviceIdType.MESH
BF = jnp.bfloat16
F32 = jnp.float32
HEADS = 32
HEAD = 32
RING = 4
HALF = 512


def wrap(v):
    return (v + RING) % RING


def place():
    d = lax.axis_index("dev")
    return d, d // 8, (d // 2) % 4, d % 2


def dev_of(y, z, c):
    return y * 8 + z * 2 + c


def dot(a, b):
    return jnp.dot(a, b, preferred_element_type=F32)


def dot_nt(a, b):
    return lax.dot_general(a, b, (((1,), (1,)), ((), ())), preferred_element_type=F32)


def dot_tn(a, b):
    return lax.dot_general(a, b, (((0,), (0,)), ((), ())), preferred_element_type=F32)


def layer_norm(values):
    average = jnp.mean(values, axis=-1, keepdims=True)
    centered = values - average
    variance = jnp.mean(centered * centered, axis=-1, keepdims=True)
    return centered / jnp.sqrt(variance + 1e-05)


def layer_kernel(
    x_hbm, wg_hbm, wqkv_hbm, inner_hbm, outer_hbm, adj_hbm, nb_hbm, blocks_hbm, counts_hbm,
    wo_hbm, wu_hbm, wd_hbm,
    o_ref,
    x, wg, w, heads, qkv, query, value, own, ring, idx, picked, inner, outsel, outin, inner_ref, outer_ref, adj, acc,
    wo, wu, wd, ob, ret, s_a, s_b, m_a, m_b, nb, blocks, counts,
    qkv_send, qkv_recv, ring_send, ring_recv, idx_send, idx_recv, pick_send, pick_recv,
    out_send, out_recv, local_sem, w_sem, ret_send, ret_recv,
):
    d, y, z, c = place()
    g = lax.axis_index("group")
    bar = pltpu.get_barrier_semaphore()

    def other(r):
        return dev_of(wrap(y + r // 8), wrap(z + (r // 2) % 4), (c + r % 2) % 2)

    def source(r):
        return dev_of(wrap(y - r // 8), wrap(z - (r // 2) % 4), (c + r % 2) % 2)

    def hail(r, carry):
        pl.semaphore_signal(bar, inc=1, device_id={"dev": other(r)}, device_id_type=MESH)
        return carry

    lax.fori_loop(1, 32, hail, 0)
    for r in range(1, 4):
        pl.semaphore_signal(bar, inc=1, device_id={"group": wrap(g + r)}, device_id_type=MESH)

    pairs = (
        (x_hbm, x), (wg_hbm, wg), (inner_hbm.at[0], inner_ref), (outer_hbm.at[0], outer_ref),
        (adj_hbm.at[0], adj.at[0, pl.ds(0, 16)]), (adj_hbm.at[1], adj.at[1, pl.ds(0, 16)]),
        (nb_hbm, nb), (blocks_hbm, blocks), (counts_hbm, counts),
        (wo_hbm, wo), (wu_hbm, wu), (wd_hbm, wd),
    )
    loads = [
        pltpu.make_async_copy(src, dst, local_sem.at[i]) for i, (src, dst) in enumerate(pairs)
    ]

    def window(n):
        return (d // 4 + 5 * n + 4) % 8

    def w_load(n, t):
        at = pl.multiple_of(t * 1024 + window(n) * 128, 128)
        return pltpu.make_async_copy(
            wqkv_hbm.at[:, pl.ds(at, 128)], w.at[n, :, pl.ds(t * 128, 128)], w_sem.at[n * 3 + t]
        )

    for load in loads[:4]:
        load.start()
    tail = jnp.where(lax.broadcasted_iota(jnp.int32, (16, 128), 0) == 0, 1.0, 0.0).astype(BF)
    for i in range(64):
        qkv[i, 96:112, :] = tail
    loads[0].wait()

    def qkv_copy(to):
        return pltpu.make_async_remote_copy(
            heads.at[to], qkv.at[pl.ds(2 * d, 2), pl.ds(0, 96)], qkv_send.at[to], qkv_recv.at[d],
            device_id={"dev": to}, device_id_type=MESH,
        )

    def qkv_land(src):
        return pltpu.make_async_remote_copy(
            heads.at[src], qkv.at[pl.ds(2 * src, 2), pl.ds(0, 96)], qkv_send.at[src], qkv_recv.at[src],
            device_id={"dev": src}, device_id_type=MESH,
        )

    def project(n, carry):
        for t in range(3):
            w_load(n, t).wait()
        turned = dot(x[...], w[n]).T.astype(BF)
        for k in range(4):
            to = window(n) * 4 + k
            for t in range(3):
                rows = turned[t * 128 + k * 32 : t * 128 + k * 32 + 32]
                for b in range(2):
                    heads[to, b, t * 32 : t * 32 + 32, :] = rows[:, b * 128 : b * 128 + 128]

            @pl.when(to != d)
            def _():
                qkv_copy(to).start()

        return carry

    loads[1].wait()
    for n in range(8):
        for t in range(3):
            w_load(n, t).start()
    for load in loads[4:9]:
        load.start()
    own[...] = dot(x[...], wg[...]).astype(BF)
    loads[2].wait()
    lists = [inner_ref[pl.ds(k, 16, 2), :] for k in range(2)]

    class Route:
        def __init__(self, h):
            self.h = h
            self.p, self.s = (z, y) if h == 0 else (y, z)

        def chip(self, p, s):
            return s * 4 + p if self.h == 0 else p * 4 + s

        def target(self, dp, ds, cc):
            return self.chip(wrap(self.p + dp), wrap(self.s + ds)) * 2 + cc

        def copies(self, tag, dp, half, to):
            v = ring.at[self.h, wrap(self.p + dp)]
            if half is not None:
                v = v.at[pl.ds(half * 128, 128)]
            k = self.h * 4 + tag
            out = [
                pltpu.make_async_remote_copy(
                    v, v, ring_send.at[k], ring_recv.at[k], device_id={"dev": to}, device_id_type=MESH
                )
            ]
            if tag < 3:
                v = idx.at[self.h, wrap(self.p + dp)]
                out.append(
                    pltpu.make_async_remote_copy(
                        v, v, idx_send.at[k], idx_recv.at[k], device_id={"dev": to}, device_id_type=MESH
                    )
                )
            return out

        def send(self, tag, dp, half, to_p):
            for copy in self.copies(tag, dp, half, self.target(to_p, 0, c)):
                copy.start()
                started.append(copy)

        def wait(self, tag, dp, half=None):
            for copy in self.copies(tag, dp, half, self.target(1, 0, c)):
                copy.wait_recv()

        def pick(self, dp, ds):
            p = wrap(self.p + dp)
            row = self.chip(self.p, wrap(self.s + ds))
            hot = jnp.where(
                lax.broadcasted_iota(jnp.int32, (256, 128), 0) == idx[self.h, p, pl.ds(row, 1), :],
                1.0, 0.0,
            ).astype(BF)
            rows = dot_tn(hot, ring[self.h, p]).astype(BF)
            for cc in range(2):
                picked[self.h, ds, cc, p] = rows[cc * 64 : cc * 64 + 64]

        def pick_copy(self, ds, dc):
            cc = (c + dc) % 2
            k = self.h * 8 + ds * 2 + dc
            return pltpu.make_async_remote_copy(
                picked.at[self.h, ds, cc], inner.at[self.h, self.s, c], pick_send.at[k], pick_recv.at[k],
                device_id={"dev": self.target(0, ds, cc)}, device_id_type=MESH,
            )

        def pick_land(self, ds, dc):
            cc = (c + dc) % 2
            k = self.h * 8 + ds * 2 + dc
            return pltpu.make_async_remote_copy(
                picked.at[self.h, ds, cc], inner.at[self.h, wrap(self.s - ds), cc],
                pick_send.at[k], pick_recv.at[k],
                device_id={"dev": self.target(0, ds, cc)}, device_id_type=MESH,
            )

    started = []
    routes = [Route(0), Route(1)]
    for t in routes:
        ring[t.h, t.p] = own[:, t.h * HALF : t.h * HALF + HALF]
        idx[t.h, t.p, :, 0:64] = lists[0]
        idx[t.h, t.p, :, 64:128] = lists[1]
    pl.semaphore_wait(bar, 34)
    for t in routes:
        t.send(0, 0, None, 1)
        t.send(1, 0, None, -1)

    lax.fori_loop(0, 8, project, 0)
    for load in loads[9:]:
        load.start()

    def outer_rows(to):
        hot = jnp.where(
            lax.broadcasted_iota(jnp.int32, (256, 128), 0) == outer_ref[pl.ds(to, 1), :], 1.0, 0.0
        ).astype(BF)
        return dot_tn(hot, own[...]).astype(BF)

    def outer_copy(r):
        return pltpu.make_async_remote_copy(
            outsel.at[r - 1], outin.at[r - 1], out_send.at[r - 1], out_recv.at[r - 1],
            device_id={"group": wrap(g + r)}, device_id_type=MESH,
        )

    loads[3].wait()
    for r in range(1, 4):
        outsel[r - 1] = outer_rows(wrap(g + r))
        outer_copy(r).start()
        started.append(outer_copy(r))

    def picks(t, count, where):
        def step(i, carry):
            t.pick(*where(i))
            return carry

        lax.fori_loop(0, count, step, 0)

    for t in routes:
        picks(t, 4, lambda i: (0 * i, i))

    def add_block(t, block):
        for b in range(2):
            at = 16
            for s in range(16):
                at = jnp.where(nb[b, s] == t, s, at)
            acc[b] += dot(adj[b, at], block)

    for i in (4, 5, 6):
        loads[i].wait()
    for b in range(2):
        adj[b, 16] = jnp.zeros((128, 128), BF)
        acc[b] = jnp.zeros((128, 1024), F32)
    add_block(0, own[0:128, :])
    add_block(1, own[128:256, :])
    add_block(18 + g, outer_rows(g))

    for t in routes:
        t.wait(0, -1)
        t.send(2, -1, 0, 1)
        t.wait(1, 1)
        t.send(3, 1, 1, -1)
    for t in routes:
        picks(t, 8, lambda i: (1 - 2 * (i // 4), i % 4))
    for t in routes:
        t.wait(2, 2, 0)
        t.wait(3, 2, 1)
        picks(t, 4, lambda i: (2 + 0 * i, i))
    for t in routes:
        inner[t.h, t.s, c] = picked[t.h, 0, c]
    for r in range(1, 4):
        outer_copy(r).wait_recv()
        add_block(18 + wrap(g - r), outin[r - 1])

    hops = [(2, 0), (2, 1), (1, 0), (1, 1), (3, 0), (3, 1), (0, 1)]
    for ds, dc in hops:
        for t in routes:
            t.pick_copy(ds, dc).start()

    qkv[pl.ds(2 * d, 2), pl.ds(0, 96)] = heads[d]

    def turn(src):
        for b in range(2):
            i = 2 * src + b
            query[i] = qkv[i, 0:32, :].astype(F32).T.astype(BF)
            value[i] = qkv[i, 64:112, :].astype(F32).T.astype(BF)

    turn(d)
    value[64] = jnp.zeros((128, 48), BF)

    def arrive(n, carry):
        src = source((5 * n) % 32)
        qkv_land(src).wait_recv()
        turn(src)
        return carry

    lax.fori_loop(1, 32, arrive, 0)
    factor = 1.4426950408889634 / HEAD**0.5
    slots = 16
    loads[7].wait()
    loads[8].wait()

    def score(i, scores, tops):
        highest = None
        for s in range(0, slots, 2):
            keys = [
                qkv[jnp.where(s + u < counts[i], blocks[s + u, i], blocks[0, i]), 32:64, :]
                for u in range(2)
            ]
            part = dot(query[i], jnp.concatenate(keys, axis=1))
            scores[:, pl.ds(s * 128, 256)] = part
            part = jnp.maximum(part[:, :128], part[:, 128:])
            highest = part if highest is None else jnp.maximum(highest, part)
        tops[...] = jnp.broadcast_to(jnp.max(highest, axis=1, keepdims=True) * factor, (128, 128))

    def mix(i, to, lanes, scores, tops):
        top = jnp.concatenate([tops[...]] * 2, axis=1)
        mixed = None
        for s in range(0, slots, 2):
            probs = jnp.exp2(scores[:, pl.ds(s * 128, 256)] * factor - top).astype(BF)
            values = [
                value[jnp.where(s + u < counts[i], blocks[s + u, i], 64)] for u in range(2)
            ]
            part = dot(probs, jnp.concatenate(values, axis=0))
            mixed = part if mixed is None else mixed + part
        mixed = mixed.T
        part = mixed[0:32] / mixed[32:33]
        ob[to, :, lanes * 128 : lanes * 128 + 128] = part.astype(BF)

    def give(r):
        return pltpu.make_async_remote_copy(
            ob.at[other(r)], ret.at[d], ret_send.at[r], ret_recv.at[r],
            device_id={"dev": other(r)}, device_id_type=MESH,
        )

    def take_in(r):
        return pltpu.make_async_remote_copy(
            ob.at[other(r)], ret.at[source(r)], ret_send.at[r], ret_recv.at[r],
            device_id={"dev": other(r)}, device_id_type=MESH,
        )

    score(other(31) * 2, s_a, m_a)

    def attend(n, carry):
        r = 31 - n
        to = other(r)
        score(to * 2 + 1, s_b, m_b)
        mix(to * 2, to, 0, s_a, m_a)
        score(other((r + 31) % 32) * 2, s_a, m_a)
        mix(to * 2 + 1, to, 1, s_b, m_b)

        @pl.when(r > 0)
        def _():
            give(r).start()

        return carry

    lax.fori_loop(0, 32, attend, 0)
    ret[d] = ob[d]

    for ds, dc in reversed(hops):
        for t in routes:
            t.pick_land(ds, dc).wait_recv()

    def gathered(row, carry):
        parts = []
        for col in range(4):
            left = inner[0, row, :, col].reshape(128, HALF)
            right = inner[1, col, :, row].reshape(128, HALF)
            parts.append(jnp.concatenate([left, right], axis=1))
        table = jnp.concatenate(parts, axis=0)
        for b in range(2):
            tiles = []
            for col in range(4):
                at = 16
                for s in range(16):
                    at = jnp.where(nb[b, s] == 2 + row * 4 + col, s, at)
                tiles.append(adj[b, at])
            acc[b] += dot(jnp.concatenate(tiles, axis=1), table)
        return carry

    lax.fori_loop(0, 4, gathered, 0)
    features = x[...].astype(F32)
    local = layer_norm(features + acc[...].reshape(256, 1024))
    loads[9].wait()

    def land(r, carry):
        take_in(r).wait_recv()
        return carry

    lax.fori_loop(1, 32, land, 0)
    projected = dot_tn(ret[...].reshape(1024, 256), wo[...])
    summed = local + layer_norm(features + projected)
    acc[...] = summed.reshape(2, 128, 1024)
    loads[10].wait()
    hidden = jax.nn.gelu(dot(summed.astype(BF), wu[...])).astype(BF)
    loads[11].wait()
    o_ref[...] = layer_norm(acc[...].reshape(256, 1024) + dot(hidden, wd[...])).astype(BF)

    for copy in started:
        copy.wait_send()
    for ds, dc in hops:
        for t in routes:
            t.pick_copy(ds, dc).wait_send()

    def leave(r, carry):
        give(r).wait_send()
        qkv_copy((d + r) % 32).wait_send()
        return carry

    lax.fori_loop(1, 32, leave, 0)


def per_device(
    node_feats, w_gcn, adj_tiles, neighbor_blocks, inner_rows, outer_rows,
    w_qkv, key_blocks, key_counts, w_out, w_up, w_down,
):
    hbm = pl.BlockSpec(memory_space=pl.ANY)
    dma = pltpu.SemaphoreType.DMA
    return pl.pallas_call(
        layer_kernel,
        out_shape=jax.ShapeDtypeStruct((256, 1024), BF),
        in_specs=[hbm] * 12,
        out_specs=pl.BlockSpec(memory_space=pltpu.VMEM),
        scratch_shapes=[
            pltpu.VMEM((256, 1024), BF),
            pltpu.VMEM((1024, 1024), BF),
            pltpu.VMEM((8, 1024, 384), BF),
            pltpu.VMEM((32, 2, 96, 128), BF),
            pltpu.VMEM((64, 112, 128), BF),
            pltpu.VMEM((64, 128, 32), BF),
            pltpu.VMEM((65, 128, 48), BF),
            pltpu.VMEM((256, 1024), BF),
            pltpu.VMEM((2, 4, 256, HALF), BF),
            pltpu.VMEM((2, 4, 16, 128), jnp.int32),
            pltpu.VMEM((2, 4, 2, 4, 64, HALF), BF),
            pltpu.VMEM((2, 4, 2, 4, 64, HALF), BF),
            pltpu.VMEM((3, 128, 1024), BF),
            pltpu.VMEM((3, 128, 1024), BF),
            pltpu.VMEM((32, 64), jnp.int32),
            pltpu.VMEM((4, 128), jnp.int32),
            pltpu.VMEM((2, 17, 128, 128), BF),
            pltpu.VMEM((2, 128, 1024), F32),
            pltpu.VMEM((1024, 1024), BF),
            pltpu.VMEM((1024, 2048), BF),
            pltpu.VMEM((2048, 1024), BF),
            pltpu.VMEM((32, 32, 256), BF),
            pltpu.VMEM((32, 32, 256), BF),
            pltpu.VMEM((128, 2048), F32),
            pltpu.VMEM((128, 2048), F32),
            pltpu.VMEM((128, 128), F32),
            pltpu.VMEM((128, 128), F32),
            pltpu.SMEM((2, 16), jnp.int32),
            pltpu.SMEM((16, 64), jnp.int32),
            pltpu.SMEM((64,), jnp.int32),
            dma((32,)), dma((32,)), dma((8,)), dma((8,)), dma((8,)), dma((8,)), dma((16,)), dma((16,)),
            dma((3,)), dma((3,)), dma((12,)), dma((24,)), dma((32,)), dma((32,)),
        ],
        compiler_params=pltpu.CompilerParams(
            collective_id=0, has_side_effects=True, vmem_limit_bytes=58 << 20
        ),
        name="layer",
    )(
        node_feats, w_gcn, w_qkv, inner_rows, outer_rows, adj_tiles, neighbor_blocks,
        key_blocks.T, key_counts, w_out, w_up, w_down,
    )


def solution(mesh):
    placed = (
        P(("group", "dev"), None),
        P(),
        P(("group", "dev"), None, None, None),
        P(("group", "dev"), None),
        P(("group", "dev"), None, None),
        P(("group", "dev"), None, None),
        P(),
        P("group", None),
        P("group"),
        P(),
        P(),
        P(),
    )
    return jax.shard_map(
        per_device, mesh=mesh, in_specs=placed, out_specs=P(("group", "dev"), None), check_vma=False
    )
```
